256 devices in a mesh: ka: 8 (over y_hi, x), band: 32 (over y_lo, z, core).
Axes of the slice: x: 4, y: 4 (y_hi: 2, y_lo: 2; y = y_hi * 2 + y_lo), z: 8, core: 2. Of those that a mesh axis runs over, the one named last changes fastest.
Arguments:
- targets: float32 [256, 2, 24, 576], P(('ka', 'band')), may hold values from -6 to 6
- occupied: bfloat16 [256, 2, 24, 576], P(('ka', 'band')), may hold values from -3 to 3
- kernels: float32 [16, 24, 576], replicated, may hold values from 0.1 to 2
- partner: int32 [8], replicated, may hold values from 0 to 7, as said below
- kernel_index: int32 [16, 16], replicated, may hold values from 0 to 15
Outputs:
- exchange: float32 [256, 2, 24, 576], P(('ka', 'band'))
The draws below stay inside these ranges and needn't reach their ends.
Inputs may be any that keep to these rules, and one draw needn't show every extreme that they name: partner is a permutation of the groups.
All inputs are finite; a program needn't handle non-finite values.
Results may differ from the reference program's by a relative error of at most 0.0003.
Values may be sent and summed in bfloat16 or wider, within the bound.
A program may use at most 64 MiB of HBM per device.

```python
import math
import jax
import jax.numpy as jnp
from jax import lax

GRID = 24
KPT_DEV = 2
NKERN = 16
NKPT = 16
NOCC_K = 16
NTGT_K = 16
N_KA = 8
N_BAND = 32


def draw_partner(key, part):
    first_key = jax.random.fold_in(key, 11)
    second_key = jax.random.fold_in(key, 23)
    order = jax.random.permutation(first_key, N_KA).astype(jnp.int32)
    chosen = jax.random.randint(second_key, (), 0, N_KA).astype(jnp.int32)
    wanted = (chosen + N_KA // 2) % N_KA
    holder = jnp.argmax(order == wanted).astype(jnp.int32)
    previous = order[chosen]
    order = order.at[holder].set(previous)
    order = order.at[chosen].set(wanted)
    return order.astype(jnp.int32)


def set_ends(drawn, rng, smallest, largest):
    shape = drawn.shape
    place = [jax.random.randint(jax.random.fold_in(rng, axis), (), 0, shape[axis]) for axis in range(len(shape))]
    drawn = drawn.at[tuple(place)].set(smallest)
    longest = shape.index(max(shape))
    place[longest] = (place[longest] + 1) % shape[longest]
    return drawn.at[tuple(place)].set(largest)


def block_scale(stream_key, dims, shards, least, largest):
    level = 1.0
    for position, shards_of in shards:
        draws = jax.random.uniform(jax.random.fold_in(jax.random.fold_in(stream_key, 6), position), (shards_of,), jnp.float32, least / len(shards), largest / len(shards))
        level = level * jnp.repeat(jnp.exp(draws), dims[position] // shards_of).reshape((-1,) + (1,) * (len(dims) - 1 - position))
    return level


def gaussian(rng, shape, width, most, cuts=(), kind=jnp.bfloat16):
    values = jax.random.normal(rng, shape, jnp.float32) * width
    if len(cuts) > 0:
        values = block_scale(rng, shape, cuts, -0.22, 0.18) * values
    return jnp.clip(values, min=-most, max=most).astype(kind)


def setup_inputs(seed: int = 0) -> dict:
    splits = jax.random.split(jax.random.key(seed), 6)
    return {
        "targets": gaussian(splits[0], (NKPT * NTGT_K, 2, GRID, GRID * GRID), 1.0, 6.0, ((0, 256),), jnp.float32),
        "occupied": gaussian(splits[1], (NKPT * NOCC_K, 2, GRID, GRID * GRID), 0.5, 3.0, ((0, 256),)),
        "kernels": jnp.clip(jnp.exp(jax.random.uniform(splits[2], (NKERN, GRID, GRID * GRID), jnp.float32, math.log(0.1), math.log(2.0))), 0.1, 2.0),
        "partner": draw_partner(jax.random.fold_in(splits[5], 71), 0),
        "kernel_index": set_ends(jax.random.randint(splits[4], (NKPT, NKPT), 0, NKERN), jax.random.fold_in(splits[4], 1), 0, NKERN - 1).astype(jnp.int32),
    }


def spectral(real_part, imag_part, inverse):
    shaped = real_part.shape[:-2] + (GRID, GRID, GRID)
    complex_field = lax.complex(real_part, imag_part).reshape(shaped)
    if inverse:
        output = jnp.fft.ifftn(complex_field, axes=(-3, -2, -1), norm="ortho")
    else:
        output = jnp.fft.fftn(complex_field, axes=(-3, -2, -1), norm="ortho")
    return jnp.real(output).reshape(real_part.shape), jnp.imag(output).reshape(real_part.shape)


def reference(targets, occupied, kernels, partner, kernel_index):
    per_kpoint = N_BAND // KPT_DEV
    group_targets = KPT_DEV * NTGT_K

    def one_group(group_number):
        partner_group = partner[group_number]
        target_block = lax.dynamic_slice_in_dim(targets, group_number * group_targets, group_targets, 0)
        occupied_block = lax.dynamic_slice_in_dim(occupied, partner_group * N_BAND, N_BAND, 0).astype(jnp.float32)
        target_k = group_number * KPT_DEV + jnp.arange(group_targets, dtype=jnp.int32) // NTGT_K
        target_real = target_block[:, 0]
        target_imag = target_block[:, 1]

        def visit(totals, visited):
            orbital, source_band = visited
            source_k = partner_group * KPT_DEV + source_band // per_kpoint
            kernel = kernels[kernel_index[target_k, source_k]]
            orbital_real = orbital[0]
            orbital_imag = orbital[1]
            dens_real = orbital_real * target_real + orbital_imag * target_imag
            dens_imag = orbital_real * target_imag - orbital_imag * target_real
            spec_real, spec_imag = spectral(dens_real, dens_imag, False)
            pot_real, pot_imag = spectral(kernel * spec_real, kernel * spec_imag, True)
            new_real = totals[0] - (orbital_real * pot_real - orbital_imag * pot_imag)
            new_imag = totals[1] - (orbital_real * pot_imag + orbital_imag * pot_real)
            return (new_real, new_imag), None

        blank = jnp.zeros(target_real.shape, jnp.float32)
        totals, unused = lax.scan(visit, (blank, blank), (occupied_block, jnp.arange(N_BAND, dtype=jnp.int32)))
        return jnp.stack(totals, axis=1)

    result = lax.map(one_group, jnp.arange(N_KA, dtype=jnp.int32))
    return result.reshape(targets.shape)
```

```python
import functools
import numpy as np
import ml_dtypes
import jax
import jax.numpy as jnp
from jax import lax
from jax.experimental import pallas as pl
from jax.experimental.pallas import tpu as pltpu

G = 24
H = 11
BF = jnp.bfloat16
F32 = jnp.float32


def point_order():
    order = np.full((5, 128), -1, np.int64)
    for t, (sb, sc) in enumerate(((1, 1), (1, -1), (-1, 1), (-1, -1))):
        for b in range(1, 12):
            for c in range(1, 12):
                order[t, (b - 1) * H + c - 1] = (sb * b % G) * G + sc * c % G
    edge = [b * G + c for b in range(G) for c in range(G) if b % 12 == 0 or c % 12 == 0]
    order[4, : len(edge)] = edge
    return order


def half_tables():
    order = point_order()
    core, edge = order[0], order[4]
    rows = np.concatenate([core, edge])
    live = rows >= 0
    b, c = rows // G, rows % G
    theta = 2 * np.pi * (np.outer(b, b) % G) / G
    phi = 2 * np.pi * (np.outer(c, c) % G) / G
    both = 2 * np.pi * ((np.outer(b, b) + np.outer(c, c)) % G) / G
    tables = np.stack([
        np.cos(theta) * np.cos(phi),
        np.cos(theta) * np.sin(phi),
        np.sin(theta) * np.cos(phi),
        -np.sin(theta) * np.sin(phi),
    ])
    tables[0, 128:, 128:] = np.cos(both)[128:, 128:]
    tables[1, 128:, 128:] = np.sin(both)[128:, 128:]
    tables[2:, 128:, 128:] = 0.0
    tables = tables * live[None, :, None] * live[None, None, :]
    high = tables.astype(ml_dtypes.bfloat16)
    low = (tables - high.astype(np.float64)).astype(ml_dtypes.bfloat16)
    return np.concatenate([high, low, high], axis=1)


def spread_table():
    order = point_order().reshape(-1)
    table = np.zeros((576, 640), np.float32)
    for lane, point in enumerate(order):
        if point >= 0:
            table[point, lane] = 1.0
    return table


def fft3(x, s3):
    (ar, ai), (br, bi), (cr, ci) = x
    tr, ti = br + cr, bi + ci
    dr, di = (br - cr) * s3, (bi - ci) * s3
    mr, mi = ar - 0.5 * tr, ai - 0.5 * ti
    return [(ar + tr, ai + ti), (mr + di, mi - dr), (mr - di, mi + dr)]


def add(x, y):
    return (x[0] + y[0], x[1] + y[1])


def sub(x, y):
    return (x[0] - y[0], x[1] - y[1])


def minus_i(x):
    return (x[1], -x[0])


def fft4(x):
    e0, e1 = add(x[0], x[2]), sub(x[0], x[2])
    o0, o1 = add(x[1], x[3]), sub(x[1], x[3])
    return [add(e0, o0), (e1[0] + o1[1], e1[1] - o1[0]), sub(e0, o0), (e1[0] - o1[1], e1[1] + o1[0])]


def fft8(x):
    r = float(np.sqrt(0.5))
    e = fft4([x[0], x[2], x[4], x[6]])
    o = fft4([x[1], x[3], x[5], x[7]])
    o1 = ((o[1][0] + o[1][1]) * r, (o[1][1] - o[1][0]) * r)
    o3 = ((o[3][1] - o[3][0]) * r, (o[3][0] + o[3][1]) * r)
    out = [None] * 8
    out[0], out[4] = add(e[0], o[0]), sub(e[0], o[0])
    out[1], out[5] = add(e[1], o1), sub(e[1], o1)
    out[2], out[6] = (e[2][0] + o[2][1], e[2][1] - o[2][0]), (e[2][0] - o[2][1], e[2][1] + o[2][0])
    out[3], out[7] = (e[3][0] + o3[0], e[3][1] - o3[1]), (e[3][0] - o3[0], e[3][1] + o3[1])
    return out


def fft24(load, store):
    s3 = float(np.sqrt(0.75))
    cols = []
    for n2 in range(8):
        cols.append(fft3([load((8 * n1 + 3 * n2) % 24) for n1 in range(3)], s3))
    for k1 in range(3):
        outs = fft8([cols[n2][k1] for n2 in range(8)])
        for k2 in range(8):
            k = next(k for k in range(24) if k % 3 == k1 and k % 8 == k2)
            store(k, outs[k2])


def split(x):
    high = x.astype(BF)
    return high, (x - high.astype(F32)).astype(BF)


R = 192


def product(xh, xl, w_ref, yc, ye):
    @pl.loop(0, 4)
    def _(p):
        left = jnp.concatenate([xh[p], xh[4], xh[p], xh[4], xl[p], xl[4]], axis=1)
        y = jnp.dot(left, w_ref[p], preferred_element_type=F32)
        yc[p] = y[:, :128]
        ye[p] = y[:, 128:]


def rows(a, n=8):
    return pl.ds(pl.multiple_of(a * 8, 8), n)


def irows(a, n=8):
    return pl.ds(pl.multiple_of(R + a * 8, 8), n)


def batch(base, kq, phi, psi, kern, w_ref, acc, xh, xl, yc, ye, z):
    def orbital(c, t, a):
        return phi[c, t, pl.ds(base * 24 + a, 8, stride=24), :]

    def spread(ref, *where):
        *lead, a = where
        return jnp.broadcast_to(ref[tuple(lead) + (pl.ds(a, 1),)], (8, 128))

    def density(t, a):
        pr, pi = orbital(0, t, a), orbital(1, t, a)
        tr, ti = spread(psi, 0, t, a), spread(psi, 1, t, a)
        return pr * tr + pi * ti, pr * ti - pi * tr

    @pl.loop(0, 12)
    def _(h):
        grid = []
        for t in range(5):
            lo = density(t, 2 * h)
            hi = density(t, 2 * h + 1)
            grid.append([jnp.concatenate([lo[c], hi[c]], axis=0) for c in range(2)])
        for c in range(2):
            pp, pm, mp, mm, edge = (grid[t][c] for t in range(5))
            s, d, u, v = pp + mm, pp - mm, pm + mp, pm - mp
            at = pl.ds(pl.multiple_of(c * R + h * 16, 16), 16)
            for p, x in enumerate((s + u, d - v, d + v, s - u, edge)):
                xh[p, at, :], xl[p, at, :] = split(x)

    product(xh, xl, w_ref, yc, ye)

    def edge_sum(a):
        er = ye[0, rows(a), :] + ye[3, rows(a), :]
        ei = ye[0, irows(a), :] + ye[3, irows(a), :]
        xr = ye[1, rows(a), :] + ye[2, rows(a), :]
        xi = ye[1, irows(a), :] + ye[2, irows(a), :]
        return er, ei, xr, xi

    def forward_edge(a):
        er, ei, xr, xi = edge_sum(a)
        return er + xi, ei - xr

    def keep(p):
        def store(k, x):
            z[p, rows(k), :] = x[0]
            z[p, irows(k), :] = x[1]
        return store

    @pl.loop(0, 4)
    def _(p):
        fft24(lambda a: (yc[p, rows(a), :], yc[p, irows(a), :]), keep(p))

    fft24(forward_edge, keep(4))

    @pl.loop(0, 24)
    def _(a):
        re = [z[p, rows(a), :] for p in range(5)]
        im = [z[p, irows(a), :] for p in range(5)]
        k = [spread(kern, kq, t, a) for t in range(5)]
        pr, qr = re[0] + re[3], re[0] - re[3]
        pi, qi = im[0] + im[3], im[0] - im[3]
        sr, dr = re[2] + re[1], re[2] - re[1]
        si, di = im[2] + im[1], im[2] - im[1]
        for out, (pp, mm, pm, mp) in enumerate((
            (pr + si, pr - si, qr + di, qr - di),
            (pi - sr, pi + sr, qi - dr, qi + dr),
        )):
            pp, pm, mp, mm = pp * k[0], pm * k[1], mp * k[2], mm * k[3]
            s, d, u, v = pp + mm, pp - mm, pm + mp, pm - mp
            at = irows(a) if out else rows(a)
            for p, x in enumerate((s + u, d - v, d + v, s - u)):
                z[p, at, :] = x
        z[4, rows(a), :] = re[4] * k[4]
        z[4, irows(a), :] = im[4] * k[4]

    @pl.loop(0, 5)
    def _(p):
        got = {}

        def store(k, x):
            got[k] = x

        fft24(lambda a: (z[p, irows(a), :], z[p, rows(a), :]), store)
        for h in range(12):
            for c in range(2):
                x = jnp.concatenate([got[2 * h][1 - c], got[2 * h + 1][1 - c]], axis=0)
                at = pl.ds(c * R + h * 16, 16)
                xh[p, at, :], xl[p, at, :] = split(x)

    product(xh, xl, w_ref, yc, ye)

    @pl.loop(0, 24)
    def _(a):
        re = [yc[p, rows(a), :] for p in range(4)]
        im = [yc[p, irows(a), :] for p in range(4)]
        pr, qr = re[0] + re[3], re[0] - re[3]
        pi, qi = im[0] + im[3], im[0] - im[3]
        sr, dr = re[2] + re[1], re[2] - re[1]
        si, di = im[2] + im[1], im[2] - im[1]
        er, ei, xr, xi = edge_sum(a)
        vr = (pr - si, qr - di, qr + di, pr + si, er - xi)
        vi = (pi + sr, qi + dr, qi - dr, pi - sr, ei + xr)
        for t in range(5):
            fr, fi = orbital(0, t, a), orbital(1, t, a)
            acc[t, rows(a), :] += fr * vr[t] - fi * vi[t]
            acc[t, irows(a), :] += fr * vi[t] + fi * vr[t]


SCRATCH = [
    pltpu.VMEM((5, 2 * R, 128), F32),
    pltpu.VMEM((5, 2 * R, 128), BF),
    pltpu.VMEM((5, 2 * R, 128), BF),
    pltpu.VMEM((4, 2 * R, 128), F32),
    pltpu.VMEM((4, 2 * R, 128), F32),
    pltpu.VMEM((5, 2 * R, 128), F32),
    pltpu.VMEM((2, 5, 768, 128), F32),
]


def local_kernel(occ_ref, psi_ref, kern_ref, w_ref, out_ref, acc, xh, xl, yc, ye, z, phi):
    acc[...] = jnp.zeros_like(acc)

    @pl.loop(0, 32)
    def _(i):
        for c in range(2):
            for t in range(5):
                phi[c, t, pl.ds(pl.multiple_of(i * 24, 8), 24), :] = occ_ref[i, c, :, t * 128:(t + 1) * 128].astype(F32)

    @pl.loop(0, 4)
    def _(n):
        batch(n * 8, n // 2, phi, psi_ref, kern_ref, w_ref, acc, xh, xl, yc, ye, z)

    for c in range(2):
        for t in range(5):
            x = acc[t, c * R:(c + 1) * R, :].reshape(24, 8, 128)
            out_ref[c, t] = jnp.sum(x, axis=1)


def compute(occ, psi, kern, w):
    return pl.pallas_call(
        local_kernel,
        out_shape=jax.ShapeDtypeStruct((2, 5, 24, 128), F32),
        in_specs=[pl.BlockSpec(memory_space=pltpu.VMEM)] * 4,
        out_specs=pl.BlockSpec(memory_space=pltpu.VMEM),
        scratch_shapes=SCRATCH,
        compiler_params=pltpu.CompilerParams(vmem_limit_bytes=60 * 2**20),
    )(occ, psi, kern, w)


KPT_DEV = 2


def spread_lanes(x, table):
    y = jnp.dot(x.reshape(-1, 576), table, precision=lax.Precision.HIGHEST, preferred_element_type=F32)
    return y.reshape(x.shape[:-1] + (5, 128))


def shards(targets, occupied, kernels, partner, kernel_index):
    per_kpoint = lax.axis_size("band") // KPT_DEV
    my_group = lax.axis_index("ka")
    kpoint = my_group * KPT_DEV + lax.axis_index("band") // per_kpoint
    table = jnp.asarray(spread_table())
    tables = jnp.asarray(half_tables())
    mine = jnp.dot(
        occupied.reshape(48, 576), table.astype(BF), preferred_element_type=F32
    ).astype(BF).reshape(1, 2, 24, 640)
    everyone = lax.all_gather(mine, "ka", axis=0, tiled=True)
    partner_group = partner[my_group]
    visitor = lax.dynamic_slice_in_dim(everyone, partner_group, 1, 0)
    occ = lax.all_gather(visitor, "band", axis=0, tiled=True)
    psi = spread_lanes(targets[0], table).transpose(0, 2, 1, 3)
    pair = lax.dynamic_slice(kernel_index, (kpoint, partner_group * KPT_DEV), (1, KPT_DEV))[0]
    kern = spread_lanes(kernels[pair] * (-1.0 / 13824.0), table).transpose(0, 2, 1, 3)
    out = compute(occ, psi, kern, tables)
    out = out.transpose(0, 2, 1, 3).reshape(48, 640)
    out = jnp.dot(out, table.T, precision=lax.Precision.HIGHEST, preferred_element_type=F32)
    return out.reshape(1, 2, 24, 576)


def solution(mesh):
    from jax.sharding import PartitionSpec as P
    return jax.shard_map(
        shards,
        mesh=mesh,
        in_specs=(P(("ka", "band"), None, None, None), P(("ka", "band"), None, None, None), P(), P(), P()),
        out_specs=P(("ka", "band"), None, None, None),
        check_vma=False,
    )
```

```python
import functools
import numpy as np
import ml_dtypes
import jax
import jax.numpy as jnp
from jax import lax
from jax.experimental import pallas as pl
from jax.experimental.pallas import tpu as pltpu

G = 24
H = 11
BF = jnp.bfloat16
F32 = jnp.float32


def point_order():
    order = np.full((5, 128), -1, np.int64)
    for t, (sb, sc) in enumerate(((1, 1), (1, -1), (-1, 1), (-1, -1))):
        for b in range(1, 12):
            for c in range(1, 12):
                order[t, (b - 1) * H + c - 1] = (sb * b % G) * G + sc * c % G
    edge = [b * G + c for b in range(G) for c in range(G) if b % 12 == 0 or c % 12 == 0]
    order[4, : len(edge)] = edge
    return order


def half_tables():
    order = point_order()
    core, edge = order[0], order[4]
    rows = np.concatenate([core, edge])
    live = rows >= 0
    b, c = rows // G, rows % G
    theta = 2 * np.pi * (np.outer(b, b) % G) / G
    phi = 2 * np.pi * (np.outer(c, c) % G) / G
    both = 2 * np.pi * ((np.outer(b, b) + np.outer(c, c)) % G) / G
    tables = np.stack([
        np.cos(theta) * np.cos(phi),
        np.cos(theta) * np.sin(phi),
        np.sin(theta) * np.cos(phi),
        -np.sin(theta) * np.sin(phi),
    ])
    tables[0, 128:, 128:] = np.cos(both)[128:, 128:]
    tables[1, 128:, 128:] = np.sin(both)[128:, 128:]
    tables[2:, 128:, 128:] = 0.0
    tables = tables * live[None, :, None] * live[None, None, :]
    high = tables.astype(ml_dtypes.bfloat16)
    low = (tables - high.astype(np.float64)).astype(ml_dtypes.bfloat16)
    return np.concatenate([high, low], axis=1)


def spread_table():
    order = point_order().reshape(-1)
    table = np.zeros((576, 640), np.float32)
    for lane, point in enumerate(order):
        if point >= 0:
            table[point, lane] = 1.0
    return table


def fft3(x, s3):
    (ar, ai), (br, bi), (cr, ci) = x
    tr, ti = br + cr, bi + ci
    dr, di = (br - cr) * s3, (bi - ci) * s3
    mr, mi = ar - 0.5 * tr, ai - 0.5 * ti
    return [(ar + tr, ai + ti), (mr + di, mi - dr), (mr - di, mi + dr)]


def add(x, y):
    return (x[0] + y[0], x[1] + y[1])


def sub(x, y):
    return (x[0] - y[0], x[1] - y[1])


def minus_i(x):
    return (x[1], -x[0])


def fft4(x):
    e0, e1 = add(x[0], x[2]), sub(x[0], x[2])
    o0, o1 = add(x[1], x[3]), sub(x[1], x[3])
    return [add(e0, o0), (e1[0] + o1[1], e1[1] - o1[0]), sub(e0, o0), (e1[0] - o1[1], e1[1] + o1[0])]


def fft8(x):
    r = float(np.sqrt(0.5))
    e = fft4([x[0], x[2], x[4], x[6]])
    o = fft4([x[1], x[3], x[5], x[7]])
    o1 = ((o[1][0] + o[1][1]) * r, (o[1][1] - o[1][0]) * r)
    o3 = ((o[3][1] - o[3][0]) * r, (o[3][0] + o[3][1]) * r)
    out = [None] * 8
    out[0], out[4] = add(e[0], o[0]), sub(e[0], o[0])
    out[1], out[5] = add(e[1], o1), sub(e[1], o1)
    out[2], out[6] = (e[2][0] + o[2][1], e[2][1] - o[2][0]), (e[2][0] - o[2][1], e[2][1] + o[2][0])
    out[3], out[7] = (e[3][0] + o3[0], e[3][1] - o3[1]), (e[3][0] - o3[0], e[3][1] + o3[1])
    return out


def fft24(load, store):
    s3 = float(np.sqrt(0.75))
    cols = []
    for n2 in range(8):
        cols.append(fft3([load((8 * n1 + 3 * n2) % 24) for n1 in range(3)], s3))
    for k1 in range(3):
        outs = fft8([cols[n2][k1] for n2 in range(8)])
        for k2 in range(8):
            k = next(k for k in range(24) if k % 3 == k1 and k % 8 == k2)
            store(k, outs[k2])


def split(x):
    high = x.astype(BF)
    return high, (x - high.astype(F32)).astype(BF)


R = 192


def product(xh, xl, w_ref, yc, ye):
    @pl.loop(0, 4)
    def _(p):
        left = jnp.concatenate([xh[p], xh[4], xh[p], xh[4], xl[p], xl[4]], axis=1)
        right = jnp.concatenate([w_ref[p], w_ref[p, :256]], axis=0)
        y = jnp.dot(left, right, preferred_element_type=F32)
        yc[p] = y[:, :128]
        ye[p] = y[:, 128:]


def rows(a, n=8):
    return pl.ds(pl.multiple_of(a * 8, 8), n)


def irows(a, n=8):
    return pl.ds(pl.multiple_of(R + a * 8, 8), n)


def batch(n, hook, blocks, phi, psi, kern, w_ref, acc, xh, xl, yc, ye, z):

    @pl.loop(0, 8)
    def _(j):
        for r in range(3):
            for t in range(5):
                at = pl.ds(pl.multiple_of(j * 48 + r * 16, 16), 16)
                phi[t, at, :] = blocks[n * 8 + j, r * 5 + t].astype(F32)

    def orbital(c, t, a):
        return phi[t, pl.ds(c * 24 + a, 8, stride=48), :]

    def row(x):
        return jnp.broadcast_to(x, (8, 128))

    def density(t, a):
        pr, pi = orbital(0, t, a), orbital(1, t, a)
        tr, ti = row(psi[t, pl.ds(a, 1), :]), row(psi[t, pl.ds(24 + a, 1), :])
        return pr * tr + pi * ti, pr * ti - pi * tr

    @pl.loop(0, 12)
    def _(h):
        grid = []
        for t in range(5):
            lo = density(t, 2 * h)
            hi = density(t, 2 * h + 1)
            grid.append([jnp.concatenate([lo[c], hi[c]], axis=0) for c in range(2)])
        for c in range(2):
            pp, pm, mp, mm, edge = (grid[t][c] for t in range(5))
            s, d, u, v = pp + mm, pp - mm, pm + mp, pm - mp
            at = pl.ds(pl.multiple_of(c * R + h * 16, 16), 16)
            for p, x in enumerate((s + u, d - v, d + v, s - u, edge)):
                xh[p, at, :], xl[p, at, :] = split(x)

    product(xh, xl, w_ref, yc, ye)
    hook(0)

    def edge_sum(a):
        er = ye[0, rows(a), :] + ye[3, rows(a), :]
        ei = ye[0, irows(a), :] + ye[3, irows(a), :]
        xr = ye[1, rows(a), :] + ye[2, rows(a), :]
        xi = ye[1, irows(a), :] + ye[2, irows(a), :]
        return er, ei, xr, xi

    def forward_edge(a):
        er, ei, xr, xi = edge_sum(a)
        return er + xi, ei - xr

    def keep(p):
        def store(k, x):
            z[p, rows(k), :] = x[0]
            z[p, irows(k), :] = x[1]
        return store

    @pl.loop(0, 4)
    def _(p):
        fft24(lambda a: (yc[p, rows(a), :], yc[p, irows(a), :]), keep(p))

    fft24(forward_edge, keep(4))

    near = jnp.where(n < 2, 6, jnp.where(n == 2, 4, 0))
    same = lax.broadcasted_iota(jnp.int32, (8, 128), 0) < near

    @pl.loop(0, 24)
    def _(a):
        re = [z[p, rows(a), :] for p in range(5)]
        im = [z[p, irows(a), :] for p in range(5)]
        k = [jnp.where(same, row(kern[t, pl.ds(a, 1), :]), row(kern[t, pl.ds(24 + a, 1), :])) for t in range(5)]
        pr, qr = re[0] + re[3], re[0] - re[3]
        pi, qi = im[0] + im[3], im[0] - im[3]
        sr, dr = re[2] + re[1], re[2] - re[1]
        si, di = im[2] + im[1], im[2] - im[1]
        for out, (pp, mm, pm, mp) in enumerate((
            (pr + si, pr - si, qr + di, qr - di),
            (pi - sr, pi + sr, qi - dr, qi + dr),
        )):
            pp, pm, mp, mm = pp * k[0], pm * k[1], mp * k[2], mm * k[3]
            s, d, u, v = pp + mm, pp - mm, pm + mp, pm - mp
            at = irows(a) if out else rows(a)
            for p, x in enumerate((s + u, d - v, d + v, s - u)):
                z[p, at, :] = x
        z[4, rows(a), :] = re[4] * k[4]
        z[4, irows(a), :] = im[4] * k[4]

    @pl.loop(0, 5)
    def _(p):
        got = {}

        def store(k, x):
            got[k] = x

        fft24(lambda a: (z[p, irows(a), :], z[p, rows(a), :]), store)
        for h in range(12):
            for c in range(2):
                x = jnp.concatenate([got[2 * h][1 - c], got[2 * h + 1][1 - c]], axis=0)
                at = pl.ds(c * R + h * 16, 16)
                xh[p, at, :], xl[p, at, :] = split(x)

    product(xh, xl, w_ref, yc, ye)
    hook(1)

    @pl.loop(0, 24)
    def _(a):
        re = [yc[p, rows(a), :] for p in range(4)]
        im = [yc[p, irows(a), :] for p in range(4)]
        pr, qr = re[0] + re[3], re[0] - re[3]
        pi, qi = im[0] + im[3], im[0] - im[3]
        sr, dr = re[2] + re[1], re[2] - re[1]
        si, di = im[2] + im[1], im[2] - im[1]
        er, ei, xr, xi = edge_sum(a)
        vr = (pr - si, qr - di, qr + di, pr + si, er - xi)
        vi = (pi + sr, qi + dr, qi - dr, pi - sr, ei + xr)
        for t in range(5):
            fr, fi = orbital(0, t, a), orbital(1, t, a)
            acc[t, rows(a), :] += fr * vr[t] - fi * vi[t]
            acc[t, irows(a), :] += fr * vi[t] + fi * vr[t]

    hook(2)


NEAR = [0, 1, -1, 2, -2, 3, -3, 4]
CHIPS = [
    (0, 0), (0, 1), (0, -1), (1, 0),
    (0, 2), (0, -2), (0, 3), (1, 1),
    (0, -3), (0, 4), (1, -1), (1, 2),
    (1, -2), (1, 3), (1, -3), (1, 4),
]
MESH = pl.DeviceIdType.MESH


def slot(y, d, c):
    return CHIPS.index((y, d)) * 2 + c


def three_parts(x):
    high = x.astype(BF)
    rest = x - high.astype(F32)
    mid = rest.astype(BF)
    return high, mid, (rest - mid.astype(F32)).astype(BF)


def permute_exact(x, table, dims):
    total = None
    for part in three_parts(x):
        y = lax.dot_general(part, table, (dims, ((), ())), preferred_element_type=F32)
        total = y if total is None else total + y
    return total


def whole_kernel(partner_ref, index_ref, occ_ref, tgt_ref, kernels_hbm, table_hbm, w_hbm, out_ref,
                 acc, xh, xl, yc, ye, z, phi, psi, kern, w_ref, table, kernels,
                 mine, spread, stage, blocks,
                 load_sem, one_send, one_recv, two_send, two_recv, band_send, band_recv):
    me = lax.axis_index("ka")
    band = lax.axis_index("band")
    core = lax.rem(band, 2)
    zed = lax.rem(band // 2, 8)
    why = band // 16

    def at(y, zz, c):
        return (me, y * 16 + zz * 2 + c)

    below = at(why, lax.rem(zed + 7, 8), core)
    above = at(why, lax.rem(zed + 1, 8), core)
    across = at(1 - why, zed, core)
    sibling = at(why, zed, 1 - core)

    loads = [
        pltpu.make_async_copy(table_hbm, table, load_sem.at[0]),
        pltpu.make_async_copy(w_hbm, w_ref, load_sem.at[1]),
        pltpu.make_async_copy(kernels_hbm, kernels, load_sem.at[2]),
    ]
    for load in loads:
        load.start()

    barrier = pltpu.get_barrier_semaphore()
    for k in range(1, 8):
        pl.semaphore_signal(barrier, inc=1, device_id=(lax.rem(me + k, 8), band), device_id_type=MESH)
    for peer in (below, above, across, sibling):
        pl.semaphore_signal(barrier, inc=1, device_id=peer, device_id_type=MESH)

    loads[0].wait()
    own = jnp.dot(occ_ref[...], table[...], preferred_element_type=F32).astype(BF)
    for r in range(3):
        for t in range(5):
            mine[r * 5 + t] = own[r * 16:(r + 1) * 16, t * 128:(t + 1) * 128]
    mine[15] = jnp.zeros((16, 128), BF)
    spread[me] = mine[pl.ds(me * 2, 2)]

    pl.semaphore_wait(barrier, 11)

    def piece(src, dst, send, recv, k):
        return pltpu.make_async_remote_copy(
            src_ref=src, dst_ref=dst, send_sem=send.at[k], recv_sem=recv.at[k],
            device_id=(lax.rem(me + k, 8), band), device_id_type=MESH)

    first = [piece(mine.at[pl.ds(lax.rem(me + k, 8) * 2, 2)], spread.at[me], one_send, one_recv, k) for k in range(1, 8)]
    for copy in first:
        copy.start()

    acc[...] = jnp.zeros_like(acc)
    psi_all = permute_exact(tgt_ref[...], table[...], ((1,), (0,)))
    for t in range(5):
        psi[t] = psi_all[:, t * 128:(t + 1) * 128]

    for copy in first:
        copy.wait_recv()
    for g in range(8):
        stage[g] = spread[partner_ref[g]]
    blocks[0, pl.ds(me * 2, 2)] = spread[partner_ref[me]]
    second = [piece(stage.at[lax.rem(me + k, 8)], blocks.at[0, pl.ds(me * 2, 2)], two_send, two_recv, k) for k in range(1, 8)]
    for copy in second:
        copy.start()

    loads[2].wait()
    group = partner_ref[me]
    kpoint = me * 2 + why
    scaled = jnp.concatenate(
        [kernels[index_ref[kpoint, group * 2 + q]] for q in (why, 1 - why)], axis=0) * (-1.0 / 13824.0)
    kern_all = permute_exact(scaled, table[...], ((1,), (0,)))
    for t in range(5):
        kern[t] = kern_all[:, t * 128:(t + 1) * 128]
    loads[1].wait()

    sent = []

    def send(source, target, peer):
        copy = pltpu.make_async_remote_copy(
            src_ref=blocks.at[source, pl.ds(0, 15)], dst_ref=blocks.at[target, pl.ds(0, 15)],
            send_sem=band_send.at[target], recv_sem=band_recv.at[target],
            device_id=peer, device_id_type=MESH)
        copy.start()
        sent.append(target)

    def arrived(target):
        pltpu.make_async_remote_copy(
            src_ref=blocks.at[0, pl.ds(0, 15)], dst_ref=blocks.at[target, pl.ds(0, 15)],
            send_sem=band_send.at[target], recv_sem=band_recv.at[target],
            device_id=sibling, device_id_type=MESH).wait_recv()

    def pass_on(y, d):
        have = slot(y, d, 0)
        if y == 0:
            if 0 <= d <= 3:
                send(have, slot(0, d + 1, 0), below)
            if -2 <= d <= 0:
                send(have, slot(0, d - 1, 0), above)
            send(have, slot(1, d, 0), across)
        send(have, slot(y, d, 1), sibling)

    def take(*chips):
        for y, d in chips:
            arrived(slot(y, d, 0))
            pass_on(y, d)

    def need(*chips):
        for y, d in chips:
            arrived(slot(y, d, 1))

    for copy in second:
        copy.wait_recv()
    pass_on(0, 0)
    take((0, 1), (0, -1), (1, 0))
    need((0, 0), (0, 1), (0, -1), (1, 0))

    steps = {
        (0, 0): lambda: take((0, 2), (0, -2), (1, 1), (1, -1)),
        (0, 1): lambda: take((0, 3), (0, -3), (1, 2), (1, -2)),
        (0, 2): lambda: need((0, 2), (0, -2), (0, 3), (1, 1)),
        (1, 0): lambda: take((0, 4), (1, 3), (1, -3)),
        (1, 1): lambda: take((1, 4)),
        (1, 2): lambda: need((0, -3), (0, 4), (1, -1), (1, 2)),
        (2, 2): lambda: need((1, -2), (1, 3), (1, -3), (1, 4)),
    }

    @pl.loop(0, 4)
    def _(n):
        def hook(place):
            for (when, where), step in steps.items():
                if where == place:
                    pl.when(n == when)(step)

        batch(n, hook, blocks, phi, psi, kern, w_ref, acc, xh, xl, yc, ye, z)

    total = []
    for c in range(2):
        total.append(jnp.concatenate(
            [jnp.sum(acc[t, c * R:(c + 1) * R, :].reshape(24, 8, 128), axis=1) for t in range(5)], axis=1))
    out_ref[...] = permute_exact(jnp.concatenate(total, axis=0), table[...], ((1,), (1,)))

    for copy in first + second:
        copy.wait_send()
    for target in sent:
        pltpu.make_async_remote_copy(
            src_ref=blocks.at[0, pl.ds(0, 15)], dst_ref=blocks.at[target, pl.ds(0, 15)],
            send_sem=band_send.at[target], recv_sem=band_recv.at[target],
            device_id=sibling, device_id_type=MESH).wait_send()


def shards(targets, occupied, kernels, partner, kernel_index):
    vmem = pl.BlockSpec(memory_space=pltpu.VMEM)
    smem = pl.BlockSpec(memory_space=pltpu.SMEM)
    hbm = pl.BlockSpec(memory_space=pl.ANY)
    sems = pltpu.SemaphoreType.DMA
    out = pl.pallas_call(
        whole_kernel,
        out_shape=jax.ShapeDtypeStruct((48, 576), F32),
        in_specs=[smem, smem, vmem, vmem, hbm, hbm, hbm],
        out_specs=vmem,
        scratch_shapes=[
            pltpu.VMEM((5, 2 * R, 128), F32),
            pltpu.VMEM((5, 2 * R, 128), BF),
            pltpu.VMEM((5, 2 * R, 128), BF),
            pltpu.VMEM((4, 2 * R, 128), F32),
            pltpu.VMEM((4, 2 * R, 128), F32),
            pltpu.VMEM((5, 2 * R, 128), F32),
            pltpu.VMEM((5, 8 * 48, 128), F32),
            pltpu.VMEM((5, 48, 128), F32),
            pltpu.VMEM((5, 48, 128), F32),
            pltpu.VMEM((4, 512, 256), BF),
            pltpu.VMEM((576, 640), BF),
            pltpu.VMEM((16, 24, 576), F32),
            pltpu.VMEM((16, 16, 128), BF),
            pltpu.VMEM((8, 2, 16, 128), BF),
            pltpu.VMEM((8, 2, 16, 128), BF),
            pltpu.VMEM((32, 16, 16, 128), BF),
            sems((3,)), sems((8,)), sems((8,)), sems((8,)), sems((8,)), sems((32,)), sems((32,)),
        ],
        compiler_params=pltpu.CompilerParams(
            vmem_limit_bytes=56 * 2**20, collective_id=0, has_side_effects=True),
    )(
        partner, kernel_index, occupied.reshape(48, 576), targets.reshape(48, 576), kernels,
        jnp.asarray(spread_table().astype(ml_dtypes.bfloat16)), jnp.asarray(half_tables()),
    )
    return out.reshape(1, 2, 24, 576)


def solution(mesh):
    from jax.sharding import PartitionSpec as P
    return jax.shard_map(
        shards,
        mesh=mesh,
        in_specs=(P(("ka", "band"), None, None, None), P(("ka", "band"), None, None, None), P(), P(), P()),
        out_specs=P(("ka", "band"), None, None, None),
        check_vma=False,
    )
```

```python
import functools
import numpy as np
import ml_dtypes
import jax
import jax.numpy as jnp
from jax import lax
from jax.experimental import pallas as pl
from jax.experimental.pallas import tpu as pltpu

G = 24
H = 11
BF = jnp.bfloat16
F32 = jnp.float32


def point_order():
    order = np.full((5, 128), -1, np.int64)
    for t, (sb, sc) in enumerate(((1, 1), (1, -1), (-1, 1), (-1, -1))):
        for b in range(1, 12):
            for c in range(1, 12):
                order[t, (b - 1) * H + c - 1] = (sb * b % G) * G + sc * c % G
    edge = [b * G + c for b in range(G) for c in range(G) if b % 12 == 0 or c % 12 == 0]
    order[4, : len(edge)] = edge
    return order


def half_tables():
    order = point_order()
    core, edge = order[0], order[4]
    rows = np.concatenate([core, edge])
    live = rows >= 0
    b, c = rows // G, rows % G
    theta = 2 * np.pi * (np.outer(b, b) % G) / G
    phi = 2 * np.pi * (np.outer(c, c) % G) / G
    both = 2 * np.pi * ((np.outer(b, b) + np.outer(c, c)) % G) / G
    tables = np.stack([
        np.cos(theta) * np.cos(phi),
        np.cos(theta) * np.sin(phi),
        np.sin(theta) * np.cos(phi),
        -np.sin(theta) * np.sin(phi),
    ])
    tables[0, 128:, 128:] = np.cos(both)[128:, 128:]
    tables[1, 128:, 128:] = np.sin(both)[128:, 128:]
    tables[2:, 128:, 128:] = 0.0
    tables = tables * live[None, :, None] * live[None, None, :]
    high = tables.astype(ml_dtypes.bfloat16)
    low = (tables - high.astype(np.float64)).astype(ml_dtypes.bfloat16)
    return np.concatenate([high, low], axis=1)


def spread_table():
    order = point_order().reshape(-1)
    table = np.zeros((576, 640), np.float32)
    for lane, point in enumerate(order):
        if point >= 0:
            table[point, lane] = 1.0
    return table


def fft3(x, s3):
    (ar, ai), (br, bi), (cr, ci) = x
    tr, ti = br + cr, bi + ci
    dr, di = (br - cr) * s3, (bi - ci) * s3
    mr, mi = ar - 0.5 * tr, ai - 0.5 * ti
    return [(ar + tr, ai + ti), (mr + di, mi - dr), (mr - di, mi + dr)]


def add(x, y):
    return (x[0] + y[0], x[1] + y[1])


def sub(x, y):
    return (x[0] - y[0], x[1] - y[1])


def minus_i(x):
    return (x[1], -x[0])


def fft4(x):
    e0, e1 = add(x[0], x[2]), sub(x[0], x[2])
    o0, o1 = add(x[1], x[3]), sub(x[1], x[3])
    return [add(e0, o0), (e1[0] + o1[1], e1[1] - o1[0]), sub(e0, o0), (e1[0] - o1[1], e1[1] + o1[0])]


def fft8(x):
    r = float(np.sqrt(0.5))
    e = fft4([x[0], x[2], x[4], x[6]])
    o = fft4([x[1], x[3], x[5], x[7]])
    o1 = ((o[1][0] + o[1][1]) * r, (o[1][1] - o[1][0]) * r)
    o3 = ((o[3][1] - o[3][0]) * r, (o[3][0] + o[3][1]) * r)
    out = [None] * 8
    out[0], out[4] = add(e[0], o[0]), sub(e[0], o[0])
    out[1], out[5] = add(e[1], o1), sub(e[1], o1)
    out[2], out[6] = (e[2][0] + o[2][1], e[2][1] - o[2][0]), (e[2][0] - o[2][1], e[2][1] + o[2][0])
    out[3], out[7] = (e[3][0] + o3[0], e[3][1] - o3[1]), (e[3][0] - o3[0], e[3][1] + o3[1])
    return out


def fft24(load, store):
    s3 = float(np.sqrt(0.75))
    cols = []
    for n2 in range(8):
        cols.append(fft3([load((8 * n1 + 3 * n2) % 24) for n1 in range(3)], s3))
    for k1 in range(3):
        outs = fft8([cols[n2][k1] for n2 in range(8)])
        for k2 in range(8):
            k = next(k for k in range(24) if k % 3 == k1 and k % 8 == k2)
            store(k, outs[k2])


def split(x):
    high = x.astype(BF)
    return high, (x - high.astype(F32)).astype(BF)


R = 192


def rows(a, n=8):
    return pl.ds(pl.multiple_of(a * 8, 8), n)


def irows(a, n=8):
    return pl.ds(pl.multiple_of(R + a * 8, 8), n)


def batch(n, hook, blocks, phi, psi, kern, w_ref, acc, xh, xl, yc, ye, z):
    late = n // 2
    which = late * (4 - n)
    low = late * (3 - n)
    high = 1 - late * (n - 2)

    @pl.when(n < 3)
    def _():
        @pl.loop(0, 8)
        def _(j):
            from_slot = (1 - late) * (n * 4 + lax.rem(j, 4)) + late * (8 + j)
            for r in range(3):
                for t in range(5):
                    at = pl.ds(pl.multiple_of(j * 48 + r * 16, 16), 16)
                    phi[t, at, :] = blocks[from_slot, r * 5 + t].astype(F32)

    def orbital(c, t, a):
        return phi[t, pl.ds(c * 24 + a, 8, stride=48), :]

    upper = lax.broadcasted_iota(jnp.int32, (8, 128), 0) < 4

    def both(ref, t, a):
        first = jnp.broadcast_to(ref[low, t, pl.ds(a, 1), :], (8, 128))
        second = jnp.broadcast_to(ref[high, t, pl.ds(a, 1), :], (8, 128))
        return jnp.where(upper, first, second)

    def density(t, a):
        pr, pi = orbital(0, t, a), orbital(1, t, a)
        tr, ti = both(psi, t, a), both(psi, t, 24 + a)
        return pr * tr + pi * ti, pr * ti - pi * tr

    @pl.loop(0, 6)
    def _(hh):
        for h in (2 * hh, 2 * hh + 1):
            grid = []
            for t in range(5):
                lo = density(t, 2 * h)
                hi = density(t, 2 * h + 1)
                grid.append([jnp.concatenate([lo[c], hi[c]], axis=0) for c in range(2)])
            for c in range(2):
                pp, pm, mp, mm, edge = (grid[t][c] for t in range(5))
                s, d, u, v = pp + mm, pp - mm, pm + mp, pm - mp
                at = pl.ds(pl.multiple_of(c * R + h * 16, 16), 16)
                for p, x in enumerate((s + u, d - v, d + v, s - u, edge)):
                    xh[p, at, :], xl[p, at, :] = split(x)

    hook(0)

    def product(p):
        left = jnp.concatenate([xh[p], xh[4], xh[p], xh[4], xl[p], xl[4]], axis=1)
        right = jnp.concatenate([w_ref[p], w_ref[p, :256]], axis=0)
        y = jnp.dot(left, right, preferred_element_type=F32)
        yc[p] = y[:, :128]
        ye[p] = y[:, 128:]

    def edge_sum(a):
        er = ye[0, rows(a), :] + ye[3, rows(a), :]
        ei = ye[0, irows(a), :] + ye[3, irows(a), :]
        xr = ye[1, rows(a), :] + ye[2, rows(a), :]
        xi = ye[1, irows(a), :] + ye[2, irows(a), :]
        return er, ei, xr, xi

    def forward_edge(a):
        er, ei, xr, xi = edge_sum(a)
        return er + xi, ei - xr

    def keep(p):
        def store(k, x):
            z[p, rows(k), :] = x[0]
            z[p, irows(k), :] = x[1]
        return store

    for p in range(4):
        product(p)
        fft24(lambda a: (yc[p, rows(a), :], yc[p, irows(a), :]), keep(p))
    fft24(forward_edge, keep(4))
    hook(1)

    @pl.loop(0, 12)
    def _(aa):
        for a in (2 * aa, 2 * aa + 1):
            re = [z[p, rows(a), :] for p in range(5)]
            im = [z[p, irows(a), :] for p in range(5)]
            k = [both(kern, t, a) for t in range(5)]
            pr, qr = re[0] + re[3], re[0] - re[3]
            pi, qi = im[0] + im[3], im[0] - im[3]
            sr, dr = re[2] + re[1], re[2] - re[1]
            si, di = im[2] + im[1], im[2] - im[1]
            for out, (pp, mm, pm, mp) in enumerate((
                (pr + si, pr - si, qr + di, qr - di),
                (pi - sr, pi + sr, qi - dr, qi + dr),
            )):
                pp, pm, mp, mm = pp * k[0], pm * k[1], mp * k[2], mm * k[3]
                s, d, u, v = pp + mm, pp - mm, pm + mp, pm - mp
                at = irows(a) if out else rows(a)
                for p, x in enumerate((s + u, d - v, d + v, s - u)):
                    z[p, at, :] = x
            z[4, rows(a), :] = re[4] * k[4]
            z[4, irows(a), :] = im[4] * k[4]

    hook(2)

    for p in (4, 0, 1, 2, 3):
        got = {}

        def store(k, x):
            got[k] = x

        fft24(lambda a: (z[p, irows(a), :], z[p, rows(a), :]), store)
        for h in range(12):
            for c in range(2):
                x = jnp.concatenate([got[2 * h][1 - c], got[2 * h + 1][1 - c]], axis=0)
                at = pl.ds(c * R + h * 16, 16)
                xh[p, at, :], xl[p, at, :] = split(x)
        if p < 4:
            product(p)
    hook(3)

    @pl.loop(0, 8)
    def _(aa):
        for a in (3 * aa, 3 * aa + 1, 3 * aa + 2):
            re = [yc[p, rows(a), :] for p in range(4)]
            im = [yc[p, irows(a), :] for p in range(4)]
            pr, qr = re[0] + re[3], re[0] - re[3]
            pi, qi = im[0] + im[3], im[0] - im[3]
            sr, dr = re[2] + re[1], re[2] - re[1]
            si, di = im[2] + im[1], im[2] - im[1]
            er, ei, xr, xi = edge_sum(a)
            vr = (pr - si, qr - di, qr + di, pr + si, er - xi)
            vi = (pi + sr, qi + dr, qi - dr, pi - sr, ei + xr)
            for t in range(5):
                fr, fi = orbital(0, t, a), orbital(1, t, a)
                acc[which, t, rows(a), :] += fr * vr[t] - fi * vi[t]
                acc[which, t, irows(a), :] += fr * vi[t] + fi * vr[t]

    hook(4)


MESH = pl.DeviceIdType.MESH
FULL = (((1,), (0,)), ((), ()))


def permute_exact(x, table):
    high = x.astype(BF)
    rest = x - high.astype(F32)
    mid = rest.astype(BF)
    low = (rest - mid.astype(F32)).astype(BF)
    y = jnp.dot(jnp.concatenate([high, mid, low], axis=0), table, preferred_element_type=F32)
    m = x.shape[0]
    return y[:m] + y[m:2 * m] + y[2 * m:]


def whole_kernel(partner_ref, index_ref, occ_ref, tgt_ref, kernels_hbm, table_hbm, back_hbm, w_hbm, out_ref,
                 acc, xh, xl, yc, ye, z, phi, psi, kern, w_ref, table, back, kernels, far, part, came,
                 mine, everyone, blocks,
                 load_sem, one_send, one_recv, pair_send, pair_recv, band_send, band_recv):
    me = lax.axis_index("ka")
    band = lax.axis_index("band")
    core = lax.rem(band, 2)
    zed = lax.rem(band // 2, 8)
    why = band // 16

    def flip(d):
        out = 0
        for bit in (1, 2, 4):
            have = lax.rem(zed // bit, 2)
            out = out + bit * ((1 - have) if d & bit else have)
        return out

    along = {d: (me, why * 16 + flip(d) * 2 + core) for d in (1, 2, 3, 7)}
    across = (me, (1 - why) * 16 + zed * 2 + core)
    sibling = (me, band + 1 - 2 * core)
    peers = list(along.values()) + [across, sibling]

    loads = [
        pltpu.make_async_copy(table_hbm, table, load_sem.at[0]),
        pltpu.make_async_copy(w_hbm, w_ref, load_sem.at[1]),
        pltpu.make_async_copy(kernels_hbm, kernels, load_sem.at[2]),
        pltpu.make_async_copy(back_hbm, back, load_sem.at[3]),
    ]
    for load in loads:
        load.start()

    barrier = pltpu.get_barrier_semaphore()
    for k in range(1, 8):
        pl.semaphore_signal(barrier, inc=1, device_id=(lax.rem(me + k, 8), band), device_id_type=MESH)
    for peer in peers:
        pl.semaphore_signal(barrier, inc=1, device_id=peer, device_id_type=MESH)

    loads[0].wait()
    own = jnp.dot(occ_ref[...], table[...], preferred_element_type=F32).astype(BF)
    for r in range(3):
        for t in range(5):
            mine[r * 5 + t] = own[r * 16:(r + 1) * 16, t * 128:(t + 1) * 128]
    everyone[me] = mine[...]

    def set_psi(which, field):
        y = permute_exact(field, table[...])
        for t in range(5):
            psi[which, t] = y[:, t * 128:(t + 1) * 128]

    set_psi(0, tgt_ref[...])
    acc[...] = jnp.zeros_like(acc)
    pl.semaphore_wait(barrier, 7 + len(peers))

    def remote(src, dst, send_sem, recv_sem, peer):
        return pltpu.make_async_remote_copy(
            src_ref=src, dst_ref=dst, send_sem=send_sem, recv_sem=recv_sem, device_id=peer, device_id_type=MESH)

    first = [
        remote(mine, everyone.at[me], one_send.at[k], one_recv.at[k], (lax.rem(me + k, 8), band))
        for k in range(1, 8)]
    for copy in first:
        copy.start()
    swap = remote(tgt_ref, far, pair_send.at[0], pair_recv.at[0], across)
    swap.start()

    loads[2].wait()
    group = partner_ref[me]
    scaled = jnp.concatenate(
        [kernels[index_ref[me * 2 + k, group * 2 + why]] for k in (why, 1 - why)], axis=0) * (-1.0 / 13824.0)
    kern_all = permute_exact(scaled, table[...])
    for k in range(2):
        for t in range(5):
            kern[k, t] = kern_all[k * 24:(k + 1) * 24, t * 128:(t + 1) * 128]
    loads[1].wait()
    loads[3].wait()

    sent = []

    def moved(target):
        return remote(blocks.at[0], blocks.at[target], band_send.at[target], band_recv.at[target], sibling)

    def send(source, target, peer):
        remote(blocks.at[source], blocks.at[target], band_send.at[target], band_recv.at[target], peer).start()
        sent.append(target)

    def take(*chips):
        for d in chips:
            moved(2 * d).wait_recv()
            send(2 * d, 2 * d + 1, sibling)
            if d == 7:
                for e in (1, 2, 3):
                    send(14, 2 * (7 - e), along[e])

    def need(*chips):
        for d in chips:
            moved(2 * d + 1).wait_recv()

    for copy in first:
        copy.wait_recv()
    blocks[0] = everyone[partner_ref[me]]
    send(0, 1, sibling)
    for d in (1, 7, 2, 3):
        send(0, 2 * d, along[d])

    swap.wait_recv()
    set_psi(1, far[...])
    take(1)
    need(0, 1)

    def total(part_of):
        sums = []
        for c in range(2):
            tiles = []
            for t in range(5):
                x = part_of(t, c)
                tiles.append(jnp.sum(x.reshape(24, 8, 128), axis=1))
            sums.append(jnp.concatenate(tiles, axis=1))
        return jnp.concatenate(sums, axis=0)

    sub = lax.rem(lax.broadcasted_iota(jnp.int32, (R, 128), 0), 8)
    back_copy = remote(part, came, pair_send.at[1], pair_recv.at[1], across)

    def give_back():
        part[...] = total(lambda t, c: acc[2, t, c * R:(c + 1) * R, :] + jnp.where(sub < 4, 0.0, acc[0, t, c * R:(c + 1) * R, :]))
        back_copy.start()

    steps = {
        (0, 0): lambda: take(2),
        (0, 1): lambda: take(3),
        (0, 3): lambda: take(7),
        (0, 4): lambda: need(2, 3),
        (1, 0): lambda: take(6),
        (1, 1): lambda: take(5),
        (1, 3): lambda: take(4),
        (1, 4): lambda: need(4, 5, 6, 7),
        (2, 4): give_back,
    }

    @pl.loop(0, 4)
    def _(n):
        def hook(place):
            for (when, where), step in steps.items():
                if where == place:
                    pl.when(n == when)(step)

        batch(n, hook, blocks, phi, psi, kern, w_ref, acc, xh, xl, yc, ye, z)

    mixed = total(lambda t, c: acc[1, t, c * R:(c + 1) * R, :] + jnp.where(sub < 4, acc[0, t, c * R:(c + 1) * R, :], 0.0))
    back_copy.wait_recv()
    out_ref[...] = permute_exact(mixed + came[...], back[...])

    for copy in first + [swap, back_copy]:
        copy.wait_send()
    for target in sent:
        moved(target).wait_send()


def shards(targets, occupied, kernels, partner, kernel_index):
    vmem = pl.BlockSpec(memory_space=pltpu.VMEM)
    smem = pl.BlockSpec(memory_space=pltpu.SMEM)
    hbm = pl.BlockSpec(memory_space=pl.ANY)
    sems = pltpu.SemaphoreType.DMA
    table = spread_table().astype(ml_dtypes.bfloat16)
    out = pl.pallas_call(
        whole_kernel,
        out_shape=jax.ShapeDtypeStruct((48, 576), F32),
        in_specs=[smem, smem, vmem, vmem, hbm, hbm, hbm, hbm],
        out_specs=vmem,
        scratch_shapes=[
            pltpu.VMEM((3, 5, 2 * R, 128), F32),
            pltpu.VMEM((5, 2 * R, 128), BF),
            pltpu.VMEM((5, 2 * R, 128), BF),
            pltpu.VMEM((4, 2 * R, 128), F32),
            pltpu.VMEM((4, 2 * R, 128), F32),
            pltpu.VMEM((5, 2 * R, 128), F32),
            pltpu.VMEM((5, 8 * 48, 128), F32),
            pltpu.VMEM((2, 5, 48, 128), F32),
            pltpu.VMEM((2, 5, 24, 128), F32),
            pltpu.VMEM((4, 512, 256), BF),
            pltpu.VMEM((576, 640), BF),
            pltpu.VMEM((640, 576), BF),
            pltpu.VMEM((16, 24, 576), F32),
            pltpu.VMEM((48, 576), F32),
            pltpu.VMEM((48, 640), F32),
            pltpu.VMEM((48, 640), F32),
            pltpu.VMEM((15, 16, 128), BF),
            pltpu.VMEM((8, 15, 16, 128), BF),
            pltpu.VMEM((16, 15, 16, 128), BF),
            sems((4,)), sems((8,)), sems((8,)), sems((2,)), sems((2,)), sems((16,)), sems((16,)),
        ],
        compiler_params=pltpu.CompilerParams(
            vmem_limit_bytes=56 * 2**20, collective_id=0, has_side_effects=True),
    )(
        partner, kernel_index, occupied.reshape(48, 576), targets.reshape(48, 576), kernels,
        jnp.asarray(table), jnp.asarray(np.ascontiguousarray(table.T)), jnp.asarray(half_tables()),
    )
    return out.reshape(1, 2, 24, 576)


def solution(mesh):
    from jax.sharding import PartitionSpec as P
    return jax.shard_map(
        shards,
        mesh=mesh,
        in_specs=(P(("ka", "band"), None, None, None), P(("ka", "band"), None, None, None), P(), P(), P()),
        out_specs=P(("ka", "band"), None, None, None),
        check_vma=False,
    )
```

```python
import functools
import numpy as np
import ml_dtypes
import jax
import jax.numpy as jnp
from jax import lax
from jax.experimental import pallas as pl
from jax.experimental.pallas import tpu as pltpu

G = 24
H = 11
BF = jnp.bfloat16
F32 = jnp.float32


def point_order():
    order = np.full((5, 128), -1, np.int64)
    for t, (sb, sc) in enumerate(((1, 1), (1, -1), (-1, 1), (-1, -1))):
        for b in range(1, 12):
            for c in range(1, 12):
                order[t, (b - 1) * H + c - 1] = (sb * b % G) * G + sc * c % G
    edge = [b * G + c for b in range(G) for c in range(G) if b % 12 == 0 or c % 12 == 0]
    order[4, : len(edge)] = edge
    return order


def half_tables():
    order = point_order()
    core, edge = order[0], order[4]
    rows = np.concatenate([core, edge])
    live = rows >= 0
    b, c = rows // G, rows % G
    theta = 2 * np.pi * (np.outer(b, b) % G) / G
    phi = 2 * np.pi * (np.outer(c, c) % G) / G
    both = 2 * np.pi * ((np.outer(b, b) + np.outer(c, c)) % G) / G
    tables = np.stack([
        np.cos(theta) * np.cos(phi),
        np.cos(theta) * np.sin(phi),
        np.sin(theta) * np.cos(phi),
        -np.sin(theta) * np.sin(phi),
    ])
    tables[0, 128:, 128:] = np.cos(both)[128:, 128:]
    tables[1, 128:, 128:] = np.sin(both)[128:, 128:]
    tables[2:, 128:, 128:] = 0.0
    tables = tables * live[None, :, None] * live[None, None, :]
    high = tables.astype(ml_dtypes.bfloat16)
    low = (tables - high.astype(np.float64)).astype(ml_dtypes.bfloat16)
    tables = np.concatenate([high, low], axis=1)
    last = np.concatenate([high[3, :128, :128], low[3, :128, :128]], axis=1)
    tables[3] = 0
    tables[3, :128] = last
    tables[3, 128:256, :128] = last[:, :128]
    return tables


def spread_table():
    order = point_order().reshape(-1)
    table = np.zeros((576, 640), np.float32)
    for lane, point in enumerate(order):
        if point >= 0:
            table[point, lane] = 1.0
    return table


def fft3(x, s3):
    (ar, ai), (br, bi), (cr, ci) = x
    tr, ti = br + cr, bi + ci
    dr, di = (br - cr) * s3, (bi - ci) * s3
    mr, mi = ar - 0.5 * tr, ai - 0.5 * ti
    return [(ar + tr, ai + ti), (mr + di, mi - dr), (mr - di, mi + dr)]


def add(x, y):
    return (x[0] + y[0], x[1] + y[1])


def sub(x, y):
    return (x[0] - y[0], x[1] - y[1])


def minus_i(x):
    return (x[1], -x[0])


def fft4(x):
    e0, e1 = add(x[0], x[2]), sub(x[0], x[2])
    o0, o1 = add(x[1], x[3]), sub(x[1], x[3])
    return [add(e0, o0), (e1[0] + o1[1], e1[1] - o1[0]), sub(e0, o0), (e1[0] - o1[1], e1[1] + o1[0])]


def fft8(x):
    r = float(np.sqrt(0.5))
    e = fft4([x[0], x[2], x[4], x[6]])
    o = fft4([x[1], x[3], x[5], x[7]])
    o1 = ((o[1][0] + o[1][1]) * r, (o[1][1] - o[1][0]) * r)
    o3 = ((o[3][1] - o[3][0]) * r, (o[3][0] + o[3][1]) * r)
    out = [None] * 8
    out[0], out[4] = add(e[0], o[0]), sub(e[0], o[0])
    out[1], out[5] = add(e[1], o1), sub(e[1], o1)
    out[2], out[6] = (e[2][0] + o[2][1], e[2][1] - o[2][0]), (e[2][0] - o[2][1], e[2][1] + o[2][0])
    out[3], out[7] = (e[3][0] + o3[0], e[3][1] - o3[1]), (e[3][0] - o3[0], e[3][1] + o3[1])
    return out


def fft24(load, store):
    s3 = float(np.sqrt(0.75))
    cols = []
    for n2 in range(8):
        cols.append(fft3([load((8 * n1 + 3 * n2) % 24) for n1 in range(3)], s3))
    for k1 in range(3):
        outs = fft8([cols[n2][k1] for n2 in range(8)])
        for k2 in range(8):
            k = next(k for k in range(24) if k % 3 == k1 and k % 8 == k2)
            store(k, outs[k2])


def split(x):
    high = x.astype(BF)
    return high, (x - high.astype(F32)).astype(BF)


R = 192


def rows(a, n=8):
    return pl.ds(pl.multiple_of(a * 8, 8), n)


def irows(a, n=8):
    return pl.ds(pl.multiple_of(R + a * 8, 8), n)


def batch(n, hook, blocks, phi, psi, kern, w_ref, acc, xh, xl, yc, ye, z):
    late = n // 2
    kind = late * (n - 1)

    @pl.when(n < 3)
    def _():
        @pl.loop(0, 8)
        def _(j):
            from_slot = (1 - late) * (n * 4 + lax.rem(j, 4)) + late * (8 + j)
            for r in range(3):
                for t in range(5):
                    at = pl.ds(pl.multiple_of(j * 48 + r * 16, 16), 16)
                    phi[t, at, :] = blocks[from_slot, r * 5 + t].astype(F32)

    def orbital(c, t, a):
        return phi[t, pl.ds(c * 24 + a, 8, stride=48), :]

    def density(t, a):
        pr, pi = orbital(0, t, a), orbital(1, t, a)
        tr, ti = psi[kind, t, rows(a), :], psi[kind, t, irows(a), :]
        return pr * tr + pi * ti, pr * ti - pi * tr

    @pl.loop(0, 4)
    def _(hh):
        for h in (3 * hh, 3 * hh + 1, 3 * hh + 2):
            grid = []
            for t in range(5):
                lo = density(t, 2 * h)
                hi = density(t, 2 * h + 1)
                grid.append([jnp.concatenate([lo[c], hi[c]], axis=0) for c in range(2)])
            for c in range(2):
                pp, pm, mp, mm, edge = (grid[t][c] for t in range(5))
                s, d, u, v = pp + mm, pp - mm, pm + mp, pm - mp
                at = pl.ds(pl.multiple_of(c * R + h * 16, 16), 16)
                for p, x in enumerate((s + u, d - v, d + v, s - u, edge)):
                    xh[p, at, :], xl[p, at, :] = split(x)

    hook(0)

    def product(p):
        if p == 3:
            left = jnp.concatenate([xh[3], xl[3]], axis=1)
            y = jnp.dot(left, w_ref[3, :256], preferred_element_type=F32)
            yc[3] = y[:, :128] + y[:, 128:]
            return
        left = jnp.concatenate([xh[p], xh[4], xh[p], xh[4], xl[p], xl[4]], axis=1)
        right = jnp.concatenate([w_ref[p], w_ref[p, :256]], axis=0)
        y = jnp.dot(left, right, preferred_element_type=F32)
        yc[p] = y[:, :128]
        ye[p] = y[:, 128:]

    def edge_sum(a):
        xr = ye[1, rows(a), :] + ye[2, rows(a), :]
        xi = ye[1, irows(a), :] + ye[2, irows(a), :]
        return ye[0, rows(a), :], ye[0, irows(a), :], xr, xi

    def forward_edge(a):
        er, ei, xr, xi = edge_sum(a)
        return er + xi, ei - xr

    def keep(p):
        def store(k, x):
            z[p, rows(k), :] = x[0]
            z[p, irows(k), :] = x[1]
        return store

    for p in range(4):
        product(p)
        fft24(lambda a: (yc[p, rows(a), :], yc[p, irows(a), :]), keep(p))
    fft24(forward_edge, keep(4))
    hook(1)

    @pl.loop(0, 4)
    def _(aa):
        for a in (6 * aa + i for i in range(6)):
            re = [z[p, rows(a), :] for p in range(5)]
            im = [z[p, irows(a), :] for p in range(5)]
            k = [kern[kind, t, rows(a), :] for t in range(5)]
            pr, qr = re[0] + re[3], re[0] - re[3]
            pi, qi = im[0] + im[3], im[0] - im[3]
            sr, dr = re[2] + re[1], re[2] - re[1]
            si, di = im[2] + im[1], im[2] - im[1]
            for out, (pp, mm, pm, mp) in enumerate((
                (pr + si, pr - si, qr + di, qr - di),
                (pi - sr, pi + sr, qi - dr, qi + dr),
            )):
                pp, pm, mp, mm = pp * k[0], pm * k[1], mp * k[2], mm * k[3]
                s, d, u, v = pp + mm, pp - mm, pm + mp, pm - mp
                at = irows(a) if out else rows(a)
                for p, x in enumerate((s + u, d - v, d + v, s - u)):
                    z[p, at, :] = x
            z[4, rows(a), :] = re[4] * k[4]
            z[4, irows(a), :] = im[4] * k[4]

    hook(2)

    for p in (4, 0, 1, 2, 3):
        got = {}

        def store(k, x):
            place = k % 3 * 8 + k % 8
            got[place] = x
            if place % 2:
                for c in range(2):
                    y = jnp.concatenate([got[place - 1][1 - c], x[1 - c]], axis=0)
                    at = pl.ds(c * R + place // 2 * 16, 16)
                    xh[p, at, :], xl[p, at, :] = split(y)

        fft24(lambda a: (z[p, irows(a), :], z[p, rows(a), :]), store)
        if p < 4:
            product(p)
    hook(3)

    @pl.loop(0, 4)
    def _(aa):
        for a in (6 * aa + i for i in range(6)):
            b = lax.rem(a, 3) * 8 + lax.rem(a, 8)
            re = [yc[p, rows(b), :] for p in range(4)]
            im = [yc[p, irows(b), :] for p in range(4)]
            pr, qr = re[0] + re[3], re[0] - re[3]
            pi, qi = im[0] + im[3], im[0] - im[3]
            sr, dr = re[2] + re[1], re[2] - re[1]
            si, di = im[2] + im[1], im[2] - im[1]
            er, ei, xr, xi = edge_sum(b)
            vr = (pr - si, qr - di, qr + di, pr + si, er - xi)
            vi = (pi + sr, qi + dr, qi - dr, pi - sr, ei + xr)
            for t in range(5):
                fr, fi = orbital(0, t, a), orbital(1, t, a)
                acc[kind, t, rows(a), :] += fr * vr[t] - fi * vi[t]
                acc[kind, t, irows(a), :] += fr * vi[t] + fi * vr[t]

    hook(4)


MESH = pl.DeviceIdType.MESH
FULL = (((1,), (0,)), ((), ()))


def permute_exact(x, table):
    high = x.astype(BF)
    rest = x - high.astype(F32)
    mid = rest.astype(BF)
    low = (rest - mid.astype(F32)).astype(BF)
    y = jnp.dot(jnp.concatenate([high, mid, low], axis=0), table, preferred_element_type=F32)
    m = x.shape[0]
    return y[:m] + y[m:2 * m] + y[2 * m:]


def whole_kernel(partner_ref, index_ref, occ_hbm, tgt_hbm, kernels_hbm, table_hbm, back_hbm, w_hbm, out_ref,
                 acc, xh, xl, yc, ye, z, phi, psi, kern, w_ref, table, back, kernels, tgt, far, part, came,
                 everyone, blocks,
                 load_sem, one_send, one_recv, pair_send, pair_recv, band_send, band_recv):
    me = lax.axis_index("ka")
    band = lax.axis_index("band")
    core = lax.rem(band, 2)
    zed = lax.rem(band // 2, 8)
    why = band // 16

    def flip(d):
        out = 0
        for bit in (1, 2, 4):
            have = lax.rem(zed // bit, 2)
            out = out + bit * ((1 - have) if d & bit else have)
        return out

    along = {d: (me, why * 16 + flip(d) * 2 + core) for d in (1, 2, 3, 7)}
    across = (me, (1 - why) * 16 + zed * 2 + core)
    sibling = (me, band + 1 - 2 * core)
    peers = list(along.values()) + [across, sibling]

    barrier = pltpu.get_barrier_semaphore()
    for k in range(1, 8):
        pl.semaphore_signal(barrier, inc=1, device_id=(lax.rem(me + k, 8), band), device_id_type=MESH)
    for peer in peers:
        pl.semaphore_signal(barrier, inc=1, device_id=peer, device_id_type=MESH)

    loads = [
        pltpu.make_async_copy(src, dst, load_sem.at[k]) for k, (src, dst) in enumerate((
            (occ_hbm, everyone.at[me]), (tgt_hbm, tgt), (table_hbm, table),
            (w_hbm, w_ref), (kernels_hbm, kernels), (back_hbm, back)))]
    for load in loads:
        load.start()
    pl.semaphore_wait(barrier, 7 + len(peers))

    def remote(src, dst, send_sem, recv_sem, peer):
        return pltpu.make_async_remote_copy(
            src_ref=src, dst_ref=dst, send_sem=send_sem, recv_sem=recv_sem, device_id=peer, device_id_type=MESH)

    first = [
        remote(occ_hbm, everyone.at[me], one_send.at[k], one_recv.at[k], (lax.rem(me + k, 8), band))
        for k in range(1, 8)]
    for copy in first:
        copy.start()
    swap = remote(tgt_hbm, far, pair_send.at[0], pair_recv.at[0], across)
    swap.start()

    for load in loads:
        load.wait()

    def spread(refs, which, field):
        for a in range(field.shape[0]):
            for t in range(5):
                x = jnp.broadcast_to(field[a:a + 1, t * 128:(t + 1) * 128], (8, 128))
                refs[which, t, a * 8:(a + 1) * 8, :] = x
                half = slice(a * 8, a * 8 + 4) if which == 2 else slice(a * 8 + 4, a * 8 + 8)
                refs[0, t, half, :] = x[:4]

    group = partner_ref[me]
    scaled = jnp.concatenate(
        [kernels[index_ref[me * 2 + k, group * 2 + why]] for k in (why, 1 - why)], axis=0) * (-1.0 / 13824.0)
    kern_all = permute_exact(scaled, table[...])
    spread(kern, 2, kern_all[:24])
    spread(kern, 1, kern_all[24:])
    spread(psi, 2, permute_exact(tgt[...], table[...]))
    acc[...] = jnp.zeros_like(acc)

    sent = []

    def moved(target):
        return remote(blocks.at[0], blocks.at[target], band_send.at[target], band_recv.at[target], sibling)

    def send(source, target, peer):
        remote(blocks.at[source], blocks.at[target], band_send.at[target], band_recv.at[target], peer).start()
        sent.append(target)

    def take(*chips):
        for d in chips:
            moved(2 * d).wait_recv()
            send(2 * d, 2 * d + 1, sibling)
            if d == 7:
                for e in (1, 2, 3):
                    send(14, 2 * (7 - e), along[e])

    def need(*chips):
        for d in chips:
            moved(2 * d + 1).wait_recv()

    for copy in first:
        copy.wait_recv()
    own = jnp.dot(everyone[group], table[...], preferred_element_type=F32).astype(BF)
    for r in range(3):
        for t in range(5):
            blocks[0, r * 5 + t] = own[r * 16:(r + 1) * 16, t * 128:(t + 1) * 128]
    send(0, 1, sibling)
    for d in (7, 1, 2, 3):
        send(0, 2 * d, along[d])

    swap.wait_recv()
    spread(psi, 1, permute_exact(far[...], table[...]))
    take(1)
    take(7)
    need(0, 1)

    def total(kinds):
        sums = []
        for c in range(2):
            for block in range(3):
                tiles = []
                for t in range(5):
                    x = None
                    for kind, subs in kinds:
                        for s in subs:
                            y = acc[kind, t, pl.ds(c * R + block * 64 + s, 8, stride=8), :]
                            x = y if x is None else x + y
                    tiles.append(x)
                sums.append(jnp.concatenate(tiles, axis=1))
        return jnp.concatenate(sums, axis=0)

    back_copy = remote(part, came, pair_send.at[1], pair_recv.at[1], across)

    def give_back():
        part[...] = total(((0, range(4, 8)), (1, range(8))))
        back_copy.start()

    steps = {
        (0, 0): lambda: take(2),
        (0, 1): lambda: take(3),
        (0, 4): lambda: need(2, 3),
        (1, 0): lambda: take(6),
        (1, 1): lambda: take(5),
        (1, 3): lambda: take(4),
        (1, 4): lambda: need(4, 5, 6, 7),
        (2, 4): give_back,
    }

    @pl.loop(0, 4)
    def _(n):
        def hook(place):
            for (when, where), step in steps.items():
                if where == place:
                    pl.when(n == when)(step)

        batch(n, hook, blocks, phi, psi, kern, w_ref, acc, xh, xl, yc, ye, z)

    mixed = total(((0, range(4)), (2, range(8))))
    back_copy.wait_recv()
    out_ref[...] = permute_exact(mixed + came[...], back[...])

    for copy in first + [swap, back_copy]:
        copy.wait_send()
    for target in sent:
        moved(target).wait_send()


def shards(targets, occupied, kernels, partner, kernel_index):
    vmem = pl.BlockSpec(memory_space=pltpu.VMEM)
    smem = pl.BlockSpec(memory_space=pltpu.SMEM)
    hbm = pl.BlockSpec(memory_space=pl.ANY)
    sems = pltpu.SemaphoreType.DMA
    table = spread_table().astype(ml_dtypes.bfloat16)
    out = pl.pallas_call(
        whole_kernel,
        out_shape=jax.ShapeDtypeStruct((48, 576), F32),
        in_specs=[smem, smem, hbm, hbm, hbm, hbm, hbm, hbm],
        out_specs=vmem,
        scratch_shapes=[
            pltpu.VMEM((3, 5, 2 * R, 128), F32),
            pltpu.VMEM((5, 2 * R, 128), BF),
            pltpu.VMEM((5, 2 * R, 128), BF),
            pltpu.VMEM((4, 2 * R, 128), F32),
            pltpu.VMEM((4, 2 * R, 128), F32),
            pltpu.VMEM((5, 2 * R, 128), F32),
            pltpu.VMEM((5, 8 * 48, 128), F32),
            pltpu.VMEM((3, 5, 2 * R, 128), F32),
            pltpu.VMEM((3, 5, R, 128), F32),
            pltpu.VMEM((4, 512, 256), BF),
            pltpu.VMEM((576, 640), BF),
            pltpu.VMEM((640, 576), BF),
            pltpu.VMEM((16, 24, 576), F32),
            pltpu.VMEM((48, 576), F32),
            pltpu.VMEM((48, 576), F32),
            pltpu.VMEM((48, 640), F32),
            pltpu.VMEM((48, 640), F32),
            pltpu.VMEM((8, 48, 576), BF),
            pltpu.VMEM((16, 15, 16, 128), BF),
            sems((6,)), sems((8,)), sems((8,)), sems((2,)), sems((2,)), sems((16,)), sems((16,)),
        ],
        compiler_params=pltpu.CompilerParams(
            vmem_limit_bytes=56 * 2**20, collective_id=0, has_side_effects=True),
    )(
        partner, kernel_index, occupied.reshape(48, 576), targets.reshape(48, 576), kernels,
        jnp.asarray(table), jnp.asarray(np.ascontiguousarray(table.T)), jnp.asarray(half_tables()),
    )
    return out.reshape(1, 2, 24, 576)


def solution(mesh):
    from jax.sharding import PartitionSpec as P
    return jax.shard_map(
        shards,
        mesh=mesh,
        in_specs=(P(("ka", "band"), None, None, None), P(("ka", "band"), None, None, None), P(), P(), P()),
        out_specs=P(("ka", "band"), None, None, None),
        check_vma=False,
    )
```

```python
import functools
import numpy as np
import ml_dtypes
import jax
import jax.numpy as jnp
from jax import lax
from jax.experimental import pallas as pl
from jax.experimental.pallas import tpu as pltpu

G = 24
H = 11
BF = jnp.bfloat16
F32 = jnp.float32


def point_order():
    order = np.full((5, 128), -1, np.int64)
    for t, (sb, sc) in enumerate(((1, 1), (1, -1), (-1, 1), (-1, -1))):
        for b in range(1, 12):
            for c in range(1, 12):
                order[t, (b - 1) * H + c - 1] = (sb * b % G) * G + sc * c % G
    edge = [b * G + c for b in range(G) for c in range(G) if b % 12 == 0 or c % 12 == 0]
    order[4, : len(edge)] = edge
    return order


def half_tables():
    order = point_order()
    core, edge = order[0], order[4]
    rows = np.concatenate([core, edge])
    live = rows >= 0
    b, c = rows // G, rows % G
    theta = 2 * np.pi * (np.outer(b, b) % G) / G
    phi = 2 * np.pi * (np.outer(c, c) % G) / G
    both = 2 * np.pi * ((np.outer(b, b) + np.outer(c, c)) % G) / G
    tables = np.stack([
        np.cos(theta) * np.cos(phi),
        np.cos(theta) * np.sin(phi),
        np.sin(theta) * np.cos(phi),
        -np.sin(theta) * np.sin(phi),
    ])
    tables[0, 128:, 128:] = np.cos(both)[128:, 128:]
    tables[1, 128:, 128:] = np.sin(both)[128:, 128:]
    tables[2:, 128:, 128:] = 0.0
    tables = tables * live[None, :, None] * live[None, None, :]
    high = tables.astype(ml_dtypes.bfloat16)
    low = (tables - high.astype(np.float64)).astype(ml_dtypes.bfloat16)
    tables = np.concatenate([high, low], axis=1)
    last = np.concatenate([high[3, :128, :128], low[3, :128, :128]], axis=1)
    tables[3] = 0
    tables[3, :128] = last
    tables[3, 128:256, :128] = last[:, :128]
    return tables


def spread_table():
    order = point_order().reshape(-1)
    table = np.zeros((576, 640), np.float32)
    for lane, point in enumerate(order):
        if point >= 0:
            table[point, lane] = 1.0
    return table


def fft3(x, s3):
    (ar, ai), (br, bi), (cr, ci) = x
    tr, ti = br + cr, bi + ci
    dr, di = (br - cr) * s3, (bi - ci) * s3
    mr, mi = ar - 0.5 * tr, ai - 0.5 * ti
    return [(ar + tr, ai + ti), (mr + di, mi - dr), (mr - di, mi + dr)]


def add(x, y):
    return (x[0] + y[0], x[1] + y[1])


def sub(x, y):
    return (x[0] - y[0], x[1] - y[1])


def minus_i(x):
    return (x[1], -x[0])


def fft4(x):
    e0, e1 = add(x[0], x[2]), sub(x[0], x[2])
    o0, o1 = add(x[1], x[3]), sub(x[1], x[3])
    return [add(e0, o0), (e1[0] + o1[1], e1[1] - o1[0]), sub(e0, o0), (e1[0] - o1[1], e1[1] + o1[0])]


def fft8(x):
    r = float(np.sqrt(0.5))
    e = fft4([x[0], x[2], x[4], x[6]])
    o = fft4([x[1], x[3], x[5], x[7]])
    o1 = ((o[1][0] + o[1][1]) * r, (o[1][1] - o[1][0]) * r)
    o3 = ((o[3][1] - o[3][0]) * r, (o[3][0] + o[3][1]) * r)
    out = [None] * 8
    out[0], out[4] = add(e[0], o[0]), sub(e[0], o[0])
    out[1], out[5] = add(e[1], o1), sub(e[1], o1)
    out[2], out[6] = (e[2][0] + o[2][1], e[2][1] - o[2][0]), (e[2][0] - o[2][1], e[2][1] + o[2][0])
    out[3], out[7] = (e[3][0] + o3[0], e[3][1] - o3[1]), (e[3][0] - o3[0], e[3][1] + o3[1])
    return out


def fft24(load, store):
    s3 = float(np.sqrt(0.75))
    cols = []
    for n2 in range(8):
        cols.append(fft3([load((8 * n1 + 3 * n2) % 24) for n1 in range(3)], s3))
    for k1 in range(3):
        outs = fft8([cols[n2][k1] for n2 in range(8)])
        for k2 in range(8):
            k = next(k for k in range(24) if k % 3 == k1 and k % 8 == k2)
            store(k, outs[k2])


def split(x):
    high = x.astype(BF)
    return high, (x - high.astype(F32)).astype(BF)


R = 192


def rows(a, n=8):
    return pl.ds(pl.multiple_of(a * 8, 8), n)


def irows(a, n=8):
    return pl.ds(pl.multiple_of(R + a * 8, 8), n)


def batch(n, hook, blocks, phi, psi, kern, w_ref, acc, xh, xl, yc, ye, z):
    late = n // 2
    kind = late * (n - 1)

    @pl.when(n < 3)
    def _():
        @pl.loop(0, 8)
        def _(j):
            from_slot = (1 - late) * (n * 4 + lax.rem(j, 4)) + late * (8 + j)
            for r in range(3):
                for t in range(5):
                    at = pl.ds(pl.multiple_of(j * 48 + r * 16, 16), 16)
                    phi[t, at, :] = blocks[from_slot, r * 5 + t].astype(F32)

    def orbital(c, t, a):
        return phi[t, pl.ds(c * 24 + a, 8, stride=48), :]

    def density(t, a):
        pr, pi = orbital(0, t, a), orbital(1, t, a)
        tr, ti = psi[kind, t, rows(a), :], psi[kind, t, irows(a), :]
        return pr * tr + pi * ti, pr * ti - pi * tr

    @pl.loop(0, 4)
    def _(hh):
        for h in (3 * hh, 3 * hh + 1, 3 * hh + 2):
            grid = []
            for t in range(5):
                lo = density(t, 2 * h)
                hi = density(t, 2 * h + 1)
                grid.append([jnp.concatenate([lo[c], hi[c]], axis=0) for c in range(2)])
            for c in range(2):
                pp, pm, mp, mm, edge = (grid[t][c] for t in range(5))
                s, d, u, v = pp + mm, pp - mm, pm + mp, pm - mp
                at = pl.ds(pl.multiple_of(c * R + h * 16, 16), 16)
                for p, x in enumerate((s + u, d - v, d + v, s - u, edge)):
                    xh[p, at, :], xl[p, at, :] = split(x)

    hook(0)

    def product(p):
        if p == 3:
            left = jnp.concatenate([xh[3], xl[3]], axis=1)
            y = jnp.dot(left, w_ref[3, :256], preferred_element_type=F32)
            yc[3] = y[:, :128] + y[:, 128:]
            return
        left = jnp.concatenate([xh[p], xh[4], xh[p], xh[4], xl[p], xl[4]], axis=1)
        right = jnp.concatenate([w_ref[p], w_ref[p, :256]], axis=0)
        y = jnp.dot(left, right, preferred_element_type=F32)
        yc[p] = y[:, :128]
        ye[p] = y[:, 128:]

    def edge_sum(a):
        xr = ye[1, rows(a), :] + ye[2, rows(a), :]
        xi = ye[1, irows(a), :] + ye[2, irows(a), :]
        return ye[0, rows(a), :], ye[0, irows(a), :], xr, xi

    def forward_edge(a):
        er, ei, xr, xi = edge_sum(a)
        return er + xi, ei - xr

    def keep(p):
        def store(k, x):
            z[p, rows(k), :] = x[0]
            z[p, irows(k), :] = x[1]
        return store

    for p in range(4):
        product(p)
        fft24(lambda a: (yc[p, rows(a), :], yc[p, irows(a), :]), keep(p))
    fft24(forward_edge, keep(4))
    hook(1)

    @pl.loop(0, 4)
    def _(aa):
        for a in (6 * aa + i for i in range(6)):
            re = [z[p, rows(a), :] for p in range(5)]
            im = [z[p, irows(a), :] for p in range(5)]
            k = [kern[kind, t, rows(a), :] for t in range(5)]
            pr, qr = re[0] + re[3], re[0] - re[3]
            pi, qi = im[0] + im[3], im[0] - im[3]
            sr, dr = re[2] + re[1], re[2] - re[1]
            si, di = im[2] + im[1], im[2] - im[1]
            for out, (pp, mm, pm, mp) in enumerate((
                (pr + si, pr - si, qr + di, qr - di),
                (pi - sr, pi + sr, qi - dr, qi + dr),
            )):
                pp, pm, mp, mm = pp * k[0], pm * k[1], mp * k[2], mm * k[3]
                s, d, u, v = pp + mm, pp - mm, pm + mp, pm - mp
                at = irows(a) if out else rows(a)
                for p, x in enumerate((s + u, d - v, d + v, s - u)):
                    z[p, at, :] = x
            z[4, rows(a), :] = re[4] * k[4]
            z[4, irows(a), :] = im[4] * k[4]

    hook(2)

    for p in (4, 0, 1, 2, 3):
        got = {}

        def store(k, x):
            place = k % 3 * 8 + k % 8
            got[place] = x
            if place % 2:
                for c in range(2):
                    y = jnp.concatenate([got[place - 1][1 - c], x[1 - c]], axis=0)
                    at = pl.ds(c * R + place // 2 * 16, 16)
                    xh[p, at, :], xl[p, at, :] = split(y)

        fft24(lambda a: (z[p, irows(a), :], z[p, rows(a), :]), store)
        if p < 4:
            product(p)
    hook(3)

    @pl.loop(0, 4)
    def _(aa):
        for a in (6 * aa + i for i in range(6)):
            b = lax.rem(a, 3) * 8 + lax.rem(a, 8)
            re = [yc[p, rows(b), :] for p in range(4)]
            im = [yc[p, irows(b), :] for p in range(4)]
            pr, qr = re[0] + re[3], re[0] - re[3]
            pi, qi = im[0] + im[3], im[0] - im[3]
            sr, dr = re[2] + re[1], re[2] - re[1]
            si, di = im[2] + im[1], im[2] - im[1]
            er, ei, xr, xi = edge_sum(b)
            vr = (pr - si, qr - di, qr + di, pr + si, er - xi)
            vi = (pi + sr, qi + dr, qi - dr, pi - sr, ei + xr)
            for t in range(5):
                fr, fi = orbital(0, t, a), orbital(1, t, a)
                acc[kind, t, rows(a), :] += fr * vr[t] - fi * vi[t]
                acc[kind, t, irows(a), :] += fr * vi[t] + fi * vr[t]

    hook(4)


MESH = pl.DeviceIdType.MESH
FULL = (((1,), (0,)), ((), ()))


def permute_exact(x, table):
    high = x.astype(BF)
    rest = x - high.astype(F32)
    mid = rest.astype(BF)
    low = (rest - mid.astype(F32)).astype(BF)
    y = jnp.dot(jnp.concatenate([high, mid, low], axis=0), table, preferred_element_type=F32)
    m = x.shape[0]
    return y[:m] + y[m:2 * m] + y[2 * m:]


def whole_kernel(partner_ref, index_ref, occ_hbm, tgt_hbm, kernels_hbm, table_hbm, back_hbm, w_hbm, out_ref,
                 acc, xh, xl, yc, ye, z, phi, psi, kern, w_ref, table, back, kernels, tgt, far, part, came,
                 everyone, blocks,
                 load_sem, one_send, one_recv, pair_send, pair_recv, band_send, band_recv):
    me = lax.axis_index("ka")
    band = lax.axis_index("band")
    core = lax.rem(band, 2)
    zed = lax.rem(band // 2, 8)
    why = band // 16

    def flip(d):
        out = 0
        for bit in (1, 2, 4):
            have = lax.rem(zed // bit, 2)
            out = out + bit * ((1 - have) if d & bit else have)
        return out

    along = {d: (me, why * 16 + flip(d) * 2 + core) for d in (1, 2, 3, 7)}
    across = (me, (1 - why) * 16 + zed * 2 + core)
    sibling = (me, band + 1 - 2 * core)
    peers = list(along.values()) + [across, sibling]

    barrier = pltpu.get_barrier_semaphore()
    for k in range(1, 8):
        pl.semaphore_signal(barrier, inc=1, device_id=(lax.rem(me + k, 8), band), device_id_type=MESH)
    for peer in peers:
        pl.semaphore_signal(barrier, inc=1, device_id=peer, device_id_type=MESH)

    loads = [
        pltpu.make_async_copy(src, dst, load_sem.at[k]) for k, (src, dst) in enumerate((
            (occ_hbm, everyone.at[me]), (tgt_hbm, tgt), (table_hbm, table),
            (w_hbm, w_ref), (kernels_hbm, kernels), (back_hbm, back)))]
    for load in loads:
        load.start()
    pl.semaphore_wait(barrier, 7 + len(peers))

    def remote(src, dst, send_sem, recv_sem, peer):
        return pltpu.make_async_remote_copy(
            src_ref=src, dst_ref=dst, send_sem=send_sem, recv_sem=recv_sem, device_id=peer, device_id_type=MESH)

    first = [
        remote(occ_hbm, everyone.at[me], one_send.at[k], one_recv.at[k], (lax.rem(me + k, 8), band))
        for k in range(1, 8)]
    for copy in first:
        copy.start()
    swap = remote(tgt_hbm, far, pair_send.at[0], pair_recv.at[0], across)

    for load in loads:
        load.wait()

    def spread(refs, which, field):
        for a in range(field.shape[0]):
            for t in range(5):
                x = jnp.broadcast_to(field[a:a + 1, t * 128:(t + 1) * 128], (8, 128))
                refs[which, t, a * 8:(a + 1) * 8, :] = x
                half = slice(a * 8, a * 8 + 4) if which == 2 else slice(a * 8 + 4, a * 8 + 8)
                refs[0, t, half, :] = x[:4]

    group = partner_ref[me]
    scaled = jnp.concatenate(
        [kernels[index_ref[me * 2 + k, group * 2 + why]] for k in (why, 1 - why)], axis=0) * (-1.0 / 13824.0)
    kern_all = permute_exact(scaled, table[...])
    spread(kern, 2, kern_all[:24])
    spread(kern, 1, kern_all[24:])
    spread(psi, 2, permute_exact(tgt[...], table[...]))
    acc[...] = jnp.zeros_like(acc)

    sent = []

    def moved(target):
        return remote(blocks.at[0], blocks.at[target], band_send.at[target], band_recv.at[target], sibling)

    def send(source, target, peer):
        remote(blocks.at[source], blocks.at[target], band_send.at[target], band_recv.at[target], peer).start()
        sent.append(target)

    def take(*chips):
        for d in chips:
            moved(2 * d).wait_recv()
            send(2 * d, 2 * d + 1, sibling)
            if d == 7:
                for e in (1, 2, 3):
                    send(14, 2 * (7 - e), along[e])

    def need(*chips):
        for d in chips:
            moved(2 * d + 1).wait_recv()

    for copy in first:
        copy.wait_recv()
    swap.start()
    own = jnp.dot(everyone[group], table[...], preferred_element_type=F32).astype(BF)
    for r in range(3):
        for t in range(5):
            blocks[0, r * 5 + t] = own[r * 16:(r + 1) * 16, t * 128:(t + 1) * 128]
    for d in (7, 1, 2, 3):
        send(0, 2 * d, along[d])
    send(0, 1, sibling)

    take(1)
    swap.wait_recv()
    spread(psi, 1, permute_exact(far[...], table[...]))
    take(7)
    need(0, 1)

    def total(kinds):
        sums = []
        for c in range(2):
            for block in range(3):
                tiles = []
                for t in range(5):
                    x = None
                    for kind, subs in kinds:
                        for s in subs:
                            y = acc[kind, t, pl.ds(c * R + block * 64 + s, 8, stride=8), :]
                            x = y if x is None else x + y
                    tiles.append(x)
                sums.append(jnp.concatenate(tiles, axis=1))
        return jnp.concatenate(sums, axis=0)

    back_copy = remote(part, came, pair_send.at[1], pair_recv.at[1], across)

    def give_back():
        part[...] = total(((0, range(4, 8)), (1, range(8))))
        back_copy.start()

    steps = {
        (0, 0): lambda: take(2),
        (0, 1): lambda: take(3),
        (0, 4): lambda: need(2, 3),
        (1, 0): lambda: take(6),
        (1, 1): lambda: take(5),
        (1, 3): lambda: take(4),
        (1, 4): lambda: need(4, 5, 6, 7),
        (2, 4): give_back,
    }

    @pl.loop(0, 4)
    def _(n):
        def hook(place):
            for (when, where), step in steps.items():
                if where == place:
                    pl.when(n == when)(step)

        batch(n, hook, blocks, phi, psi, kern, w_ref, acc, xh, xl, yc, ye, z)

    mixed = total(((0, range(4)), (2, range(8))))
    back_copy.wait_recv()
    out_ref[...] = permute_exact(mixed + came[...], back[...])

    for copy in first + [swap, back_copy]:
        copy.wait_send()
    for target in sent:
        moved(target).wait_send()


def shards(targets, occupied, kernels, partner, kernel_index):
    vmem = pl.BlockSpec(memory_space=pltpu.VMEM)
    smem = pl.BlockSpec(memory_space=pltpu.SMEM)
    hbm = pl.BlockSpec(memory_space=pl.ANY)
    sems = pltpu.SemaphoreType.DMA
    table = spread_table().astype(ml_dtypes.bfloat16)
    out = pl.pallas_call(
        whole_kernel,
        out_shape=jax.ShapeDtypeStruct((48, 576), F32),
        in_specs=[smem, smem, hbm, hbm, hbm, hbm, hbm, hbm],
        out_specs=vmem,
        scratch_shapes=[
            pltpu.VMEM((3, 5, 2 * R, 128), F32),
            pltpu.VMEM((5, 2 * R, 128), BF),
            pltpu.VMEM((5, 2 * R, 128), BF),
            pltpu.VMEM((4, 2 * R, 128), F32),
            pltpu.VMEM((4, 2 * R, 128), F32),
            pltpu.VMEM((5, 2 * R, 128), F32),
            pltpu.VMEM((5, 8 * 48, 128), F32),
            pltpu.VMEM((3, 5, 2 * R, 128), F32),
            pltpu.VMEM((3, 5, R, 128), F32),
            pltpu.VMEM((4, 512, 256), BF),
            pltpu.VMEM((576, 640), BF),
            pltpu.VMEM((640, 576), BF),
            pltpu.VMEM((16, 24, 576), F32),
            pltpu.VMEM((48, 576), F32),
            pltpu.VMEM((48, 576), F32),
            pltpu.VMEM((48, 640), F32),
            pltpu.VMEM((48, 640), F32),
            pltpu.VMEM((8, 48, 576), BF),
            pltpu.VMEM((16, 15, 16, 128), BF),
            sems((6,)), sems((8,)), sems((8,)), sems((2,)), sems((2,)), sems((16,)), sems((16,)),
        ],
        compiler_params=pltpu.CompilerParams(
            vmem_limit_bytes=56 * 2**20, collective_id=0, has_side_effects=True),
    )(
        partner, kernel_index, occupied.reshape(48, 576), targets.reshape(48, 576), kernels,
        jnp.asarray(table), jnp.asarray(np.ascontiguousarray(table.T)), jnp.asarray(half_tables()),
    )
    return out.reshape(1, 2, 24, 576)


def solution(mesh):
    from jax.sharding import PartitionSpec as P
    return jax.shard_map(
        shards,
        mesh=mesh,
        in_specs=(P(("ka", "band"), None, None, None), P(("ka", "band"), None, None, None), P(), P(), P()),
        out_specs=P(("ka", "band"), None, None, None),
        check_vma=False,
    )
```

```python
import functools
import numpy as np
import ml_dtypes
import jax
import jax.numpy as jnp
from jax import lax
from jax.experimental import pallas as pl
from jax.experimental.pallas import tpu as pltpu

G = 24
H = 11
BF = jnp.bfloat16
F32 = jnp.float32


def point_order():
    order = np.full((5, 128), -1, np.int64)
    for t, (sb, sc) in enumerate(((1, 1), (1, -1), (-1, 1), (-1, -1))):
        for b in range(1, 12):
            for c in range(1, 12):
                order[t, (b - 1) * H + c - 1] = (sb * b % G) * G + sc * c % G
    edge = [b * G + c for b in range(G) for c in range(G) if b % 12 == 0 or c % 12 == 0]
    order[4, : len(edge)] = edge
    return order


def half_tables():
    order = point_order()
    core, edge = order[0], order[4]
    rows = np.concatenate([core, edge])
    live = rows >= 0
    b, c = rows // G, rows % G
    theta = 2 * np.pi * (np.outer(b, b) % G) / G
    phi = 2 * np.pi * (np.outer(c, c) % G) / G
    both = 2 * np.pi * ((np.outer(b, b) + np.outer(c, c)) % G) / G
    tables = np.stack([
        np.cos(theta) * np.cos(phi),
        np.cos(theta) * np.sin(phi),
        np.sin(theta) * np.cos(phi),
        -np.sin(theta) * np.sin(phi),
    ])
    tables[0, 128:, 128:] = np.cos(both)[128:, 128:]
    tables[1, 128:, 128:] = np.sin(both)[128:, 128:]
    tables[2:, 128:, 128:] = 0.0
    tables = tables * live[None, :, None] * live[None, None, :]
    high = tables.astype(ml_dtypes.bfloat16)
    low = (tables - high.astype(np.float64)).astype(ml_dtypes.bfloat16)
    tables = np.concatenate([high, low], axis=1)
    last = np.concatenate([high[3, :128, :128], low[3, :128, :128]], axis=1)
    tables[3] = 0
    tables[3, :128] = last
    tables[3, 128:256, :128] = last[:, :128]
    return tables


def spread_table():
    order = point_order().reshape(-1)
    table = np.zeros((576, 640), np.float32)
    for lane, point in enumerate(order):
        if point >= 0:
            table[point, lane] = 1.0
    return table


def fft3(x, s3):
    (ar, ai), (br, bi), (cr, ci) = x
    tr, ti = br + cr, bi + ci
    dr, di = (br - cr) * s3, (bi - ci) * s3
    mr, mi = ar - 0.5 * tr, ai - 0.5 * ti
    return [(ar + tr, ai + ti), (mr + di, mi - dr), (mr - di, mi + dr)]


def add(x, y):
    return (x[0] + y[0], x[1] + y[1])


def sub(x, y):
    return (x[0] - y[0], x[1] - y[1])


def minus_i(x):
    return (x[1], -x[0])


def fft4(x):
    e0, e1 = add(x[0], x[2]), sub(x[0], x[2])
    o0, o1 = add(x[1], x[3]), sub(x[1], x[3])
    return [add(e0, o0), (e1[0] + o1[1], e1[1] - o1[0]), sub(e0, o0), (e1[0] - o1[1], e1[1] + o1[0])]


def fft8(x):
    r = float(np.sqrt(0.5))
    e = fft4([x[0], x[2], x[4], x[6]])
    o = fft4([x[1], x[3], x[5], x[7]])
    o1 = ((o[1][0] + o[1][1]) * r, (o[1][1] - o[1][0]) * r)
    o3 = ((o[3][1] - o[3][0]) * r, (o[3][0] + o[3][1]) * r)
    out = [None] * 8
    out[0], out[4] = add(e[0], o[0]), sub(e[0], o[0])
    out[1], out[5] = add(e[1], o1), sub(e[1], o1)
    out[2], out[6] = (e[2][0] + o[2][1], e[2][1] - o[2][0]), (e[2][0] - o[2][1], e[2][1] + o[2][0])
    out[3], out[7] = (e[3][0] + o3[0], e[3][1] - o3[1]), (e[3][0] - o3[0], e[3][1] + o3[1])
    return out


def fft24(load, store):
    s3 = float(np.sqrt(0.75))
    cols = []
    for n2 in range(8):
        cols.append(fft3([load((8 * n1 + 3 * n2) % 24) for n1 in range(3)], s3))
    for k1 in range(3):
        outs = fft8([cols[n2][k1] for n2 in range(8)])
        for k2 in range(8):
            k = next(k for k in range(24) if k % 3 == k1 and k % 8 == k2)
            store(k, outs[k2])


def split(x):
    high = x.astype(BF)
    return high, (x - high.astype(F32)).astype(BF)


R = 192


def rows(a, n=8):
    return pl.ds(pl.multiple_of(a * 8, 8), n)


def irows(a, n=8):
    return pl.ds(pl.multiple_of(R + a * 8, 8), n)


def batch(n, hook, blocks, phi, psi, kern, w_ref, acc, xh, xl, yc, ye, z):
    late = n // 2
    kind = late * (n - 1)

    @pl.when(n < 3)
    def _():
        @pl.loop(0, 8)
        def _(j):
            from_slot = (1 - late) * (n * 4 + lax.rem(j, 4)) + late * (8 + j)
            for r in range(3):
                for t in range(5):
                    at = pl.ds(pl.multiple_of(j * 48 + r * 16, 16), 16)
                    phi[t, at, :] = blocks[from_slot, r * 5 + t].astype(F32)

    def orbital(c, t, a):
        return phi[t, pl.ds(c * 24 + a, 8, stride=48), :]

    def density(t, a):
        pr, pi = orbital(0, t, a), orbital(1, t, a)
        tr, ti = psi[kind, t, rows(a), :], psi[kind, t, irows(a), :]
        return pr * tr + pi * ti, pr * ti - pi * tr

    @pl.loop(0, 4)
    def _(hh):
        for h in (3 * hh, 3 * hh + 1, 3 * hh + 2):
            grid = []
            for t in range(5):
                lo = density(t, 2 * h)
                hi = density(t, 2 * h + 1)
                grid.append([jnp.concatenate([lo[c], hi[c]], axis=0) for c in range(2)])
            for c in range(2):
                pp, pm, mp, mm, edge = (grid[t][c] for t in range(5))
                s, d, u, v = pp + mm, pp - mm, pm + mp, pm - mp
                at = pl.ds(pl.multiple_of(c * R + h * 16, 16), 16)
                for p, x in enumerate((s + u, d - v, d + v, s - u, edge)):
                    xh[p, at, :], xl[p, at, :] = split(x)

    hook(0)

    def product(p):
        if p == 3:
            left = jnp.concatenate([xh[3], xl[3]], axis=1)
            y = jnp.dot(left, w_ref[3, :256], preferred_element_type=F32)
            yc[3] = y[:, :128] + y[:, 128:]
            return
        left = jnp.concatenate([xh[p], xh[4], xh[p], xh[4], xl[p], xl[4]], axis=1)
        right = jnp.concatenate([w_ref[p], w_ref[p, :256]], axis=0)
        y = jnp.dot(left, right, preferred_element_type=F32)
        yc[p] = y[:, :128]
        ye[p] = y[:, 128:]

    def edge_sum(a):
        xr = ye[1, rows(a), :] + ye[2, rows(a), :]
        xi = ye[1, irows(a), :] + ye[2, irows(a), :]
        return ye[0, rows(a), :], ye[0, irows(a), :], xr, xi

    def forward_edge(a):
        er, ei, xr, xi = edge_sum(a)
        return er + xi, ei - xr

    def keep(p):
        def store(k, x):
            z[p, rows(k), :] = x[0]
            z[p, irows(k), :] = x[1]
        return store

    for p in range(4):
        product(p)
        fft24(lambda a: (yc[p, rows(a), :], yc[p, irows(a), :]), keep(p))
    fft24(forward_edge, keep(4))
    hook(1)

    @pl.loop(0, 4)
    def _(aa):
        for a in (6 * aa + i for i in range(6)):
            re = [z[p, rows(a), :] for p in range(5)]
            im = [z[p, irows(a), :] for p in range(5)]
            k = [kern[kind, t, rows(a), :] for t in range(5)]
            pr, qr = re[0] + re[3], re[0] - re[3]
            pi, qi = im[0] + im[3], im[0] - im[3]
            sr, dr = re[2] + re[1], re[2] - re[1]
            si, di = im[2] + im[1], im[2] - im[1]
            for out, (pp, mm, pm, mp) in enumerate((
                (pr + si, pr - si, qr + di, qr - di),
                (pi - sr, pi + sr, qi - dr, qi + dr),
            )):
                pp, pm, mp, mm = pp * k[0], pm * k[1], mp * k[2], mm * k[3]
                s, d, u, v = pp + mm, pp - mm, pm + mp, pm - mp
                at = irows(a) if out else rows(a)
                for p, x in enumerate((s + u, d - v, d + v, s - u)):
                    z[p, at, :] = x
            z[4, rows(a), :] = re[4] * k[4]
            z[4, irows(a), :] = im[4] * k[4]

    hook(2)

    for p in (4, 0, 1, 2, 3):
        got = {}

        def store(k, x):
            place = k % 3 * 8 + k % 8
            got[place] = x
            if place % 2:
                for c in range(2):
                    y = jnp.concatenate([got[place - 1][1 - c], x[1 - c]], axis=0)
                    at = pl.ds(c * R + place // 2 * 16, 16)
                    xh[p, at, :], xl[p, at, :] = split(y)

        fft24(lambda a: (z[p, irows(a), :], z[p, rows(a), :]), store)
        if p < 4:
            product(p)
    hook(3)

    @pl.loop(0, 4)
    def _(aa):
        for a in (6 * aa + i for i in range(6)):
            b = lax.rem(a, 3) * 8 + lax.rem(a, 8)
            re = [yc[p, rows(b), :] for p in range(4)]
            im = [yc[p, irows(b), :] for p in range(4)]
            pr, qr = re[0] + re[3], re[0] - re[3]
            pi, qi = im[0] + im[3], im[0] - im[3]
            sr, dr = re[2] + re[1], re[2] - re[1]
            si, di = im[2] + im[1], im[2] - im[1]
            er, ei, xr, xi = edge_sum(b)
            vr = (pr - si, qr - di, qr + di, pr + si, er - xi)
            vi = (pi + sr, qi + dr, qi - dr, pi - sr, ei + xr)
            for t in range(5):
                fr, fi = orbital(0, t, a), orbital(1, t, a)
                acc[kind, t, rows(a), :] += fr * vr[t] - fi * vi[t]
                acc[kind, t, irows(a), :] += fr * vi[t] + fi * vr[t]

    hook(4)


MESH = pl.DeviceIdType.MESH
FULL = (((1,), (0,)), ((), ()))


def permute_exact(x, table):
    high = x.astype(BF)
    rest = x - high.astype(F32)
    mid = rest.astype(BF)
    low = (rest - mid.astype(F32)).astype(BF)
    y = jnp.dot(jnp.concatenate([high, mid, low], axis=0), table, preferred_element_type=F32)
    m = x.shape[0]
    return y[:m] + y[m:2 * m] + y[2 * m:]


def whole_kernel(partner_ref, index_ref, occ_hbm, tgt_hbm, kernels_hbm, table_hbm, back_hbm, w_hbm, out_ref,
                 acc, xh, xl, yc, ye, z, phi, psi, kern, w_ref, table, back, kernels, tgt, far, part, came,
                 everyone, blocks,
                 load_sem, one_send, one_recv, pair_send, pair_recv, band_send, band_recv):
    me = lax.axis_index("ka")
    band = lax.axis_index("band")
    core = lax.rem(band, 2)
    zed = lax.rem(band // 2, 8)
    why = band // 16

    def flip(d):
        out = 0
        for bit in (1, 2, 4):
            have = lax.rem(zed // bit, 2)
            out = out + bit * ((1 - have) if d & bit else have)
        return out

    along = {d: (me, why * 16 + flip(d) * 2 + core) for d in (1, 2, 3, 7)}
    across = (me, (1 - why) * 16 + zed * 2 + core)
    sibling = (me, band + 1 - 2 * core)
    peers = list(along.values()) + [across, sibling]

    barrier = pltpu.get_barrier_semaphore()
    for k in range(1, 8):
        pl.semaphore_signal(barrier, inc=1, device_id=(lax.rem(me + k, 8), band), device_id_type=MESH)
    for peer in peers:
        pl.semaphore_signal(barrier, inc=1, device_id=peer, device_id_type=MESH)

    loads = [
        pltpu.make_async_copy(src, dst, load_sem.at[k]) for k, (src, dst) in enumerate((
            (occ_hbm, everyone.at[me]), (tgt_hbm, tgt), (table_hbm, table),
            (w_hbm, w_ref), (kernels_hbm, kernels), (back_hbm, back)))]
    for load in loads:
        load.start()
    pl.semaphore_wait(barrier, 7 + len(peers))

    def remote(src, dst, send_sem, recv_sem, peer):
        return pltpu.make_async_remote_copy(
            src_ref=src, dst_ref=dst, send_sem=send_sem, recv_sem=recv_sem, device_id=peer, device_id_type=MESH)

    first = [
        remote(occ_hbm, everyone.at[me], one_send.at[k], one_recv.at[k], (lax.rem(me + k, 8), band))
        for k in range(1, 8)]
    for copy in first:
        copy.start()
    swap = remote(tgt_hbm, far, pair_send.at[0], pair_recv.at[0], across)

    for load in loads:
        load.wait()

    def spread(refs, which, field):
        for a in range(field.shape[0]):
            for t in range(5):
                x = jnp.broadcast_to(field[a:a + 1, t * 128:(t + 1) * 128], (8, 128))
                refs[which, t, a * 8:(a + 1) * 8, :] = x
                half = slice(a * 8, a * 8 + 4) if which == 2 else slice(a * 8 + 4, a * 8 + 8)
                refs[0, t, half, :] = x[:4]

    group = partner_ref[me]
    scaled = jnp.concatenate(
        [kernels[index_ref[me * 2 + k, group * 2 + why]] for k in (why, 1 - why)], axis=0) * (-1.0 / 13824.0)
    kern_all = permute_exact(scaled, table[...])
    spread(kern, 2, kern_all[:24])
    spread(kern, 1, kern_all[24:])
    spread(psi, 2, permute_exact(tgt[...], table[...]))
    acc[...] = jnp.zeros_like(acc)

    sent = []

    def moved(target):
        return remote(blocks.at[0], blocks.at[target], band_send.at[target], band_recv.at[target], sibling)

    def send(source, target, peer):
        remote(blocks.at[source], blocks.at[target], band_send.at[target], band_recv.at[target], peer).start()
        sent.append(target)

    def take(*chips):
        for d in chips:
            moved(2 * d).wait_recv()
            send(2 * d, 2 * d + 1, sibling)
            if d == 7:
                for e in (1, 2, 3):
                    send(14, 2 * (7 - e), along[e])

    def need(*chips):
        for d in chips:
            moved(2 * d + 1).wait_recv()

    for copy in first:
        copy.wait_recv()
    swap.start()
    own = jnp.dot(everyone[group], table[...], preferred_element_type=F32).astype(BF)
    for r in range(3):
        for t in range(5):
            blocks[0, r * 5 + t] = own[r * 16:(r + 1) * 16, t * 128:(t + 1) * 128]
    for d in (7, 1, 2, 3):
        send(0, 2 * d, along[d])
    send(0, 1, sibling)

    take(1)
    swap.wait_recv()
    spread(psi, 1, permute_exact(far[...], table[...]))
    take(7)
    need(0, 1)

    def total(kinds):
        sums = []
        for c in range(2):
            for block in range(3):
                tiles = []
                for t in range(5):
                    x = None
                    for kind, subs in kinds:
                        for s in subs:
                            y = acc[kind, t, pl.ds(c * R + block * 64 + s, 8, stride=8), :]
                            x = y if x is None else x + y
                    tiles.append(x)
                sums.append(jnp.concatenate(tiles, axis=1))
        return jnp.concatenate(sums, axis=0)

    back_copy = remote(part, came, pair_send.at[1], pair_recv.at[1], across)

    def give_back():
        part[...] = total(((0, range(4, 8)), (1, range(8))))
        back_copy.start()

    steps = {
        (0, 0): lambda: take(2),
        (0, 1): lambda: take(3),
        (0, 4): lambda: (need(2, 3), take(6))[0],
        (1, 0): lambda: take(5),
        (1, 1): lambda: take(4),
        (1, 4): lambda: need(4, 5, 6, 7),
        (2, 4): give_back,
    }

    @pl.loop(0, 4)
    def _(n):
        def hook(place):
            for (when, where), step in steps.items():
                if where == place:
                    pl.when(n == when)(step)

        batch(n, hook, blocks, phi, psi, kern, w_ref, acc, xh, xl, yc, ye, z)

    mixed = total(((0, range(4)), (2, range(8))))
    back_copy.wait_recv()
    out_ref[...] = permute_exact(mixed + came[...], back[...])

    for copy in first + [swap, back_copy]:
        copy.wait_send()
    for target in sent:
        moved(target).wait_send()


def shards(targets, occupied, kernels, partner, kernel_index):
    vmem = pl.BlockSpec(memory_space=pltpu.VMEM)
    smem = pl.BlockSpec(memory_space=pltpu.SMEM)
    hbm = pl.BlockSpec(memory_space=pl.ANY)
    sems = pltpu.SemaphoreType.DMA
    table = spread_table().astype(ml_dtypes.bfloat16)
    out = pl.pallas_call(
        whole_kernel,
        out_shape=jax.ShapeDtypeStruct((48, 576), F32),
        in_specs=[smem, smem, hbm, hbm, hbm, hbm, hbm, hbm],
        out_specs=vmem,
        scratch_shapes=[
            pltpu.VMEM((3, 5, 2 * R, 128), F32),
            pltpu.VMEM((5, 2 * R, 128), BF),
            pltpu.VMEM((5, 2 * R, 128), BF),
            pltpu.VMEM((4, 2 * R, 128), F32),
            pltpu.VMEM((4, 2 * R, 128), F32),
            pltpu.VMEM((5, 2 * R, 128), F32),
            pltpu.VMEM((5, 8 * 48, 128), F32),
            pltpu.VMEM((3, 5, 2 * R, 128), F32),
            pltpu.VMEM((3, 5, R, 128), F32),
            pltpu.VMEM((4, 512, 256), BF),
            pltpu.VMEM((576, 640), BF),
            pltpu.VMEM((640, 576), BF),
            pltpu.VMEM((16, 24, 576), F32),
            pltpu.VMEM((48, 576), F32),
            pltpu.VMEM((48, 576), F32),
            pltpu.VMEM((48, 640), F32),
            pltpu.VMEM((48, 640), F32),
            pltpu.VMEM((8, 48, 576), BF),
            pltpu.VMEM((16, 15, 16, 128), BF),
            sems((6,)), sems((8,)), sems((8,)), sems((2,)), sems((2,)), sems((16,)), sems((16,)),
        ],
        compiler_params=pltpu.CompilerParams(
            vmem_limit_bytes=56 * 2**20, collective_id=0, has_side_effects=True),
    )(
        partner, kernel_index, occupied.reshape(48, 576), targets.reshape(48, 576), kernels,
        jnp.asarray(table), jnp.asarray(np.ascontiguousarray(table.T)), jnp.asarray(half_tables()),
    )
    return out.reshape(1, 2, 24, 576)


def solution(mesh):
    from jax.sharding import PartitionSpec as P
    return jax.shard_map(
        shards,
        mesh=mesh,
        in_specs=(P(("ka", "band"), None, None, None), P(("ka", "band"), None, None, None), P(), P(), P()),
        out_specs=P(("ka", "band"), None, None, None),
        check_vma=False,
    )
```
